256 devices in a mesh: blk: 4 (over x_hi, core), rows: 64 (over x_lo, y, z).
Axes of the slice: x: 4 (x_hi: 2, x_lo: 2; x = x_hi * 2 + x_lo), y: 4, z: 8, core: 2. Of those that a mesh axis runs over, the one named last changes fastest.
Arguments:
- fock_band: bfloat16 [65536, 2176], P('rows'), may hold values from -0.125 to 0.125
- fock_slot_mask: int32 [512, 17], P('rows'), may hold values from 0 to 1, as said below
- orbital_slab: bfloat16 [65536, 2048], P('rows', 'blk'), may hold values from -16 to 16
- orbital_mask: int32 [512, 16], P('rows', 'blk'), may hold values 0 or 1
- result_mask: int32 [512, 16], P('rows', 'blk'), may hold values 0 or 1
Outputs:
- product_slab: bfloat16 [65536, 2048], P('rows', 'blk')
- projected: float32 [2048, 2048], P('rows', 'blk')
The draws below stay inside these ranges and needn't reach their ends.
Inputs may be any that keep to these rules, and one draw needn't show every extreme that they name: `fock_slot_mask`: 1 marks a present block slot.
All inputs are finite; a program needn't handle non-finite values. No bound on the sum of `orbital_mask` or of `result_mask` on one device may be relied on, other than what follows from the above.
Results may differ from the reference program's by a relative error of at most 0.0029.
Values may be sent and summed in bfloat16 or wider, within the bound.
No kernel may reach another device: no remote copies, remote signals or barrier semaphores. Data moves between devices by JAX's collectives and lax.ppermute only.
A program may use at most 64 MiB of HBM per device.

```python
import math
import jax
import jax.numpy as jnp
from jax import lax

BLOCK = 128
BAND = 17
NB = 512
ORDER = 65536
SLAB = 2048


def draw_fock_slot_mask(key, part):
    levels = jax.random.randint(key, (NB, BAND), 0, 64)
    row_position = lax.broadcasted_iota(jnp.int32, (NB, BAND), 0)
    row_limit = 16 + 48 * row_position // NB
    return (levels < row_limit).astype(jnp.int32)


def plant(array, key, least, top_value):
    longest = array.shape.index(max(array.shape))
    spots = []
    for shift in (0, 1):
        where = [jax.random.randint(jax.random.fold_in(key, axis), (), 0, length) for axis, length in enumerate(array.shape)]
        where[longest] = (where[longest] + shift) % array.shape[longest]
        spots.append(tuple(where))
    return array.at[spots[0]].set(least).at[spots[1]].set(top_value)


def spiked(result, stream_key, source, target, shards_of, factor):
    def block_of(position):
        return (jnp.arange(result.shape[position]) // (result.shape[position] // shards_of)).reshape((-1,) + (1,) * (result.ndim - 1 - position))

    near = jax.random.permutation(stream_key, shards_of)[block_of(target)]
    second = (block_of(target) + shards_of // 2) % shards_of
    return jnp.where((block_of(source) == near) | (block_of(source) == second), factor * result, result)


def block_scale(own_key, shape, cuts, smallest, high):
    gain, own = 1.0, jax.random.fold_in(own_key, 6)
    for dim, shards_of in cuts:
        draws = jnp.exp(jax.random.uniform(jax.random.fold_in(own, dim), (shards_of,), jnp.float32, smallest / len(cuts), high / len(cuts)))
        gain = gain * jnp.repeat(draws, shape[dim] // shards_of).reshape([-1 if axis == dim else 1 for axis in range(len(shape))])
    return gain


def bell_draw(rng, extent, width, reach, shards=(), dtype=jnp.bfloat16):
    result = width * jax.random.normal(rng, extent, jnp.float32)
    if shards:
        result = result * block_scale(rng, extent, shards, -0.22, 0.18)
    return jnp.clip(result, -reach, reach).astype(dtype)


def heavy_noise(key, shape, deviation, most, pieces, heavy, kind=jnp.bfloat16):
    array = deviation * jax.random.normal(key, shape, jnp.float32)
    if pieces:
        array = array * block_scale(key, shape, pieces, -0.22, 0.18)
    return jnp.clip(spiked(array, jax.random.fold_in(key, 3), *heavy), -most, most).astype(kind)


def setup_inputs(seed: int = 0) -> dict:
    arg_keys = jax.random.split(jax.random.key(seed), 6)
    fock_band = bell_draw(arg_keys[0], (ORDER, BAND * BLOCK), (BAND * BLOCK) ** -0.5, 0.125, ((0, 64),))
    fock_slot_mask = draw_fock_slot_mask(jax.random.fold_in(arg_keys[5], 71), 0)
    orbital_slab = heavy_noise(arg_keys[2], (ORDER, SLAB), 1.0, 16.0, ((0, 64), (1, 4)), (0, 1, 64, 4.0))
    orbital_mask = plant((jax.random.randint(arg_keys[3], (NB, SLAB // BLOCK), 0, 4) < 3).astype(jnp.int32), jax.random.fold_in(arg_keys[3], 1), 0, 1)
    result_mask = plant((jax.random.randint(arg_keys[4], (NB, SLAB // BLOCK), 0, 4) < 3).astype(jnp.int32), jax.random.fold_in(arg_keys[4], 1), 0, 1)
    return dict(fock_band=fock_band, fock_slot_mask=fock_slot_mask, orbital_slab=orbital_slab, orbital_mask=orbital_mask, result_mask=result_mask)


def reference(fock_band, fock_slot_mask, orbital_slab, orbital_mask, result_mask):
    radius = (BAND - 1) // 2
    col_blocks = SLAB // BLOCK
    fock_block_list = fock_band.reshape(NB, BLOCK, BAND, BLOCK) * fock_slot_mask[:, None, :, None].astype(jnp.bfloat16)
    slab_blocks = (orbital_slab.reshape(NB, BLOCK, col_blocks, BLOCK) * orbital_mask[:, None, :, None].astype(jnp.bfloat16)).reshape(NB, BLOCK, SLAB)
    summed_total = jnp.zeros((NB, BLOCK, SLAB), jnp.float32)
    for band_shift in range(BAND):
        band_window = jnp.roll(slab_blocks, radius - band_shift, axis=0)
        summed_total = summed_total + jnp.einsum('wnq,wqg->wng', fock_block_list[:, :, band_shift, :].astype(jnp.float32), band_window.astype(jnp.float32))
    product_slab = (summed_total.reshape(NB, BLOCK, col_blocks, BLOCK) * result_mask[:, None, :, None].astype(jnp.float32)).reshape(NB * BLOCK, SLAB).astype(jnp.bfloat16)
    slab_rows = slab_blocks.reshape(NB * BLOCK, SLAB)
    projected = jnp.dot(slab_rows.T, product_slab, preferred_element_type=jnp.float32) * (1.0 / math.sqrt(NB * BLOCK))
    return (product_slab, projected)
```

```python
import functools
import math

import jax
import jax.numpy as jnp
from jax import lax
from jax.experimental import pallas as pl
from jax.experimental.pallas import tpu as pltpu
from jax.sharding import Mesh, PartitionSpec as P

F32, BF16 = jnp.float32, jnp.bfloat16
ROWS = ("xl", "y", "z")
BLK = ("xh", "core")
VMEM = pl.BlockSpec(memory_space=pltpu.VMEM)
SMEM = pl.BlockSpec(memory_space=pltpu.SMEM)
MIB = 1 << 20


def call(body, outs, ins, scratch=(), limit=24 * MIB, flops=0, moved=0):
    return pl.pallas_call(
        body,
        out_shape=outs,
        in_specs=ins,
        out_specs=jax.tree.map(lambda _: VMEM, outs),
        scratch_shapes=list(scratch),
        compiler_params=pltpu.CompilerParams(vmem_limit_bytes=limit),
        cost_estimate=pl.CostEstimate(flops=flops, bytes_accessed=moved, transcendentals=0),
    )


def mask_kernel(size, mask_ref, slab_ref, out_ref):
    blocks, panels = mask_ref.shape
    for i in range(blocks):
        for j in range(panels):
            at = (pl.ds(i * size, size), pl.ds(j * size, size))
            tile = slab_ref[at]
            out_ref[at] = jnp.where(mask_ref[i, j] != 0, tile, jnp.zeros_like(tile))


def product_kernel(size, fmask_ref, rmask_ref, fock_ref, low_ref, mid_ref, high_ref, out_ref, outt_ref, held):
    blocks, slots = fmask_ref.shape
    panels = rmask_ref.shape[1]
    for i in range(blocks):
        rows = pl.ds(i * size, size)
        for o in range(slots):
            tile = fock_ref[rows, pl.ds(o * size, size)]
            held[i % 2, :, pl.ds(o * size, size)] = jnp.where(
                fmask_ref[i, o] != 0, tile, jnp.zeros_like(tile)
            )
        first, last = (blocks - i) * size, (2 * blocks - i) * size
        fock = held.at[i % 2]
        total = jnp.dot(fock[:, first:last], mid_ref[...], preferred_element_type=F32)
        total += jnp.dot(fock[:, :first], low_ref[i * size :, :], preferred_element_type=F32)
        total += jnp.dot(
            fock[:, last:], high_ref[: (i + 1) * size, :], preferred_element_type=F32
        )
        for j in range(panels):
            cols = slice(j * size, (j + 1) * size)
            tile = total[:, cols]
            tile = jnp.where(rmask_ref[i, j] != 0, tile, jnp.zeros_like(tile)).astype(BF16)
            out_ref[rows, cols] = tile
            outt_ref[cols, rows] = tile.T


def project_kernel(panel_ref, prodt_ref, own_ref, core_ref, far_ref, both_ref, out_ref):
    half = out_ref.shape[2]
    for q, ref in enumerate((own_ref, core_ref, far_ref, both_ref)):
        terms = jnp.dot(prodt_ref[...], ref[...], preferred_element_type=F32).astype(BF16)
        where = (panel_ref[0] ^ q) * 2
        out_ref[where] = terms[:, :half]
        out_ref[where + 1] = terms[:, half:]


def first_sum_kernel(in_ref, out_ref):
    total = in_ref[0].astype(F32)
    for s in range(1, in_ref.shape[0]):
        total += in_ref[s].astype(F32)
    out_ref[...] = total.T.astype(BF16)


def last_sum_kernel(factor, in_ref, out_ref):
    total = in_ref[0].astype(F32)
    for s in range(1, in_ref.shape[0]):
        total += in_ref[s].astype(F32)
    out_ref[...] = total * factor


def ring(count, step):
    return [(i, (i + step) % count) for i in range(count)]


def on_device(fock_band, fock_slot_mask, orbital_slab, orbital_mask, result_mask):
    blocks, slots = fock_slot_mask.shape
    rows, columns = orbital_slab.shape
    size = rows // blocks
    like = functools.partial(jax.ShapeDtypeStruct)
    slab = call(functools.partial(mask_kernel, size), like((rows, columns), BF16), [SMEM, VMEM])(
        orbital_mask, orbital_slab
    )
    groups = lax.axis_size(ROWS)
    low = lax.ppermute(slab, ROWS, ring(groups, 1))
    high = lax.ppermute(slab, ROWS, ring(groups, groups - 1))
    far = lax.ppermute(slab, "xh", ring(2, 1))
    near = lax.ppermute(slab, "core", ring(2, 1))
    both = lax.ppermute(far, "core", ring(2, 1))
    product, flipped = call(
        functools.partial(product_kernel, size),
        (like((rows, columns), BF16), like((columns, rows), BF16)),
        [SMEM, SMEM, VMEM, VMEM, VMEM, VMEM],
        [pltpu.VMEM((2, size, slots * size), BF16)],
        flops=2 * rows * slots * size * columns,
        moved=2 * rows * (slots * size + 5 * columns),
    )(fock_slot_mask, result_mask, fock_band, low, slab, high)
    panel = (lax.axis_index("xh") * 2 + lax.axis_index("core")).reshape(1)
    outer = lax.axis_size("xl") * lax.axis_size("y")
    inner = lax.axis_size("z")
    chunk = columns * 4 // outer
    terms = call(
        project_kernel,
        like((outer, columns, chunk), BF16),
        [SMEM, VMEM, VMEM, VMEM, VMEM, VMEM],
        flops=8 * rows * columns * columns,
        moved=2 * 9 * rows * columns,
    )(panel, flipped, slab, near, far, both)
    terms = lax.all_to_all(terms, ("xl", "y"), 0, 0, tiled=True)
    part = call(first_sum_kernel, like((chunk, columns), BF16), [VMEM])(terms)
    part = part.reshape(inner, chunk // inner, columns)
    part = lax.all_to_all(part, "z", 0, 0, tiled=True)
    factor = 1.0 / math.sqrt(rows * groups)
    projected = call(
        functools.partial(last_sum_kernel, factor),
        like((chunk // inner, columns), F32),
        [VMEM],
    )(part)
    return (product, projected)


def solution(mesh):
    split = Mesh(mesh.devices.reshape(2, 2, 2, 4, 8), BLK + ROWS)
    placed = (P(ROWS, None), P(ROWS, None), P(ROWS, BLK), P(ROWS, BLK), P(ROWS, BLK))
    return jax.shard_map(
        on_device,
        mesh=split,
        in_specs=placed,
        out_specs=(P(ROWS, BLK), P(ROWS, BLK)),
        check_vma=False,
    )
```

```python
import functools
import math

import jax
import jax.numpy as jnp
from jax import lax
from jax.experimental import pallas as pl
from jax.experimental.pallas import tpu as pltpu
from jax.sharding import Mesh, PartitionSpec as P

F32, BF16 = jnp.float32, jnp.bfloat16
ROWS = ("xl", "y", "z")
BLK = ("xh", "core")
VMEM = pl.BlockSpec(memory_space=pltpu.VMEM)
SMEM = pl.BlockSpec(memory_space=pltpu.SMEM)
MIB = 1 << 20


def call(body, outs, ins, scratch=(), limit=8 * MIB, flops=0, moved=0):
    return pl.pallas_call(
        body,
        out_shape=outs,
        in_specs=ins,
        out_specs=jax.tree.map(lambda _: VMEM, outs),
        scratch_shapes=list(scratch),
        compiler_params=pltpu.CompilerParams(vmem_limit_bytes=limit),
        cost_estimate=pl.CostEstimate(flops=flops, bytes_accessed=moved, transcendentals=0),
    )


def dot(a, b):
    return jnp.dot(a, b, preferred_element_type=F32)


def mask_kernel(size, mask_ref, slab_ref, out_ref, h0_ref, h1_ref):
    panels, blocks = mask_ref.shape
    half = panels // 2
    for j in range(panels):
        ref = (h0_ref, h1_ref)[j // half]
        for i in range(blocks):
            rows = pl.ds(i * size, size)
            tile = slab_ref[rows, pl.ds(j * size, size)]
            tile = jnp.where(mask_ref[j, i] != 0, tile, jnp.zeros_like(tile))
            ref[rows, pl.ds((j % half) * size, size)] = tile
            out_ref[rows, pl.ds(j * size, size)] = tile


def middle_kernel(size, fmask_ref, fock_ref, h0_ref, h1_ref, held_ref, m0_ref, m1_ref, token_ref):
    token_ref[...] = jnp.zeros_like(token_ref)
    blocks, slots = fmask_ref.shape
    for i in range(blocks):
        rows = pl.ds(i * size, size)
        for o in range(slots):
            cols = pl.ds(o * size, size)
            tile = fock_ref[rows, cols]
            held_ref[rows, cols] = jnp.where(fmask_ref[i, o] != 0, tile, jnp.zeros_like(tile))
        fock = held_ref[rows, pl.ds((blocks - i) * size, blocks * size)]
        m0_ref[rows, :] = dot(fock, h0_ref[...])
        m1_ref[rows, :] = dot(fock, h1_ref[...])


def near_kernel(size, h, core_ref, y_ref, rmask_ref, held_ref, mid_ref, low_ref, high_ref, own_ref, near_ref, *rest):
    start = 0
    if h == 1:
        first_ref, opposite_ref, rest = rest[0], rest[1], rest[2:]
        start = first_ref.shape[1]
    out_ref, outt_ref, s0, s1, s2, s3 = rest
    if h == 1:
        out_ref[:, :start] = first_ref[...]
        s2[:start, :] = opposite_ref[...]
    blocks = rmask_ref.shape[1]
    slots = held_ref.shape[1] // size
    panels = mid_ref.shape[1] // size
    for i in range(blocks):
        rows = pl.ds(i * size, size)
        total = mid_ref[rows, :]
        total += dot(held_ref[rows, : (blocks - i) * size], low_ref[i * size :, :])
        total += dot(held_ref[rows, (2 * blocks - i) * size :], high_ref[: (slots - 2 * blocks + i) * size, :])
        for j in range(panels):
            cols = slice(j * size, (j + 1) * size)
            tile = total[:, cols]
            keep = rmask_ref[h * panels + j, i] != 0
            tile = jnp.where(keep, tile, jnp.zeros_like(tile)).astype(BF16)
            out_ref[rows, pl.ds(start + j * size, size)] = tile
            outt_ref[cols, rows] = tile.T
    project(core_ref, y_ref, outt_ref, own_ref, near_ref, (s0, s1, s2.at[pl.ds(start, s0.shape[0]), :], s3))


def project(core_ref, y_ref, outt_ref, same_ref, other_ref, to):
    half = to[0].shape[1]
    for q, ref in enumerate((same_ref, other_ref)):
        for k in range(2):
            terms = dot(outt_ref[...], ref[:, pl.ds(k * half, half)])
            step = ((core_ref[0] ^ q) * 2 + k - y_ref[0] + 4) % 4
            for s, into in enumerate(to):

                @pl.when(step == s)
                def _():
                    into[...] = terms.astype(into.dtype)


def far_kernel(core_ref, y_ref, t0_ref, t1_ref, far_ref, both_ref, *to):
    half = t0_ref.shape[0]
    for k, t in enumerate((t0_ref, t1_ref)):
        project(core_ref, y_ref, t, far_ref, both_ref, [ref.at[pl.ds(k * half, half), :] for ref in to])


def first_sum_kernel(xh_ref, own0, up0, down0, own1, up1, down1, opposite, far, up, cross, down, out_ref):
    count, deep, columns = out_ref.shape
    inner = count // 2
    half = own0.shape[0]
    lower, upper = pl.ds(0, half), pl.ds(half, half)

    def emit(first, cols, *parts):
        total = parts[0]
        for part in parts[1:]:
            total += part.astype(F32)
        turned = total.T.astype(BF16)
        for z in range(inner):
            out_ref[first + z, :, cols] = turned[z * deep : (z + 1) * deep]

    first = xh_ref[0] * inner
    emit(first, lower, own0[...], up0[...], down0[...], opposite[lower, :])
    emit(first, upper, own1[...], up1[...], down1[...], opposite[upper, :])
    first = (1 - xh_ref[0]) * inner
    for cols in (lower, upper):
        emit(first, cols, far[cols, :], up[cols, :], cross[cols, :], down[cols, :])


def last_sum_kernel(factor, in_ref, out_ref):
    total = in_ref[0].astype(F32)
    for s in range(1, in_ref.shape[0]):
        total += in_ref[s].astype(F32)
    out_ref[...] = total * factor


def after(x, *others):
    anywhere = pl.BlockSpec(memory_space=pl.ANY)
    return pl.pallas_call(
        lambda *refs: None,
        out_shape=jax.ShapeDtypeStruct(x.shape, x.dtype),
        in_specs=[anywhere] * (1 + len(others)),
        out_specs=anywhere,
        input_output_aliases={0: 0},
        compiler_params=pltpu.CompilerParams(vmem_limit_bytes=MIB),
    )(x, *others)


def ring(count, step):
    return [(i, (i + step) % count) for i in range(count)]


def on_device(fock_band, fock_slot_mask, orbital_slab, orbital_mask, result_mask):
    blocks, slots = fock_slot_mask.shape
    rows, columns = orbital_slab.shape
    size = rows // blocks
    half = columns // 2
    like = jax.ShapeDtypeStruct
    groups, inner = lax.axis_size(ROWS), lax.axis_size("z")
    xh, core, y = (lax.axis_index(name).reshape(1) for name in ("xh", "core", "y"))
    piece = like((rows, half), BF16)
    slab, h0, h1 = call(
        functools.partial(mask_kernel, size), (like((rows, columns), BF16), piece, piece), [SMEM, VMEM]
    )(orbital_mask.T, orbital_slab)
    up, down, swap = ring(groups, 1), ring(groups, groups - 1), ring(2, 1)
    low0, high0 = lax.ppermute(h0, ROWS, up), lax.ppermute(h0, ROWS, down)
    near_slab = lax.ppermute(slab, "core", swap)
    far_slab = lax.ppermute(slab, "xh", swap)
    held, mid0, mid1, token = call(
        functools.partial(middle_kernel, size),
        (like((rows, slots * size), BF16), *[like((rows, half), F32)] * 2, like((8, size), F32)),
        [SMEM, VMEM, VMEM, VMEM],
        flops=2 * rows * rows * columns,
        moved=4 * rows * slots * size,
    )(fock_slot_mask, fock_band, h0, h1)
    h1 = after(h1, low0, high0, token)
    low1, high1 = lax.ppermute(h1, ROWS, up), lax.ppermute(h1, ROWS, down)
    term, own = like((half, half), BF16), like((half, half), F32)
    long, long_own = like((columns, half), BF16), like((columns, half), F32)
    flipped = like((half, rows), BF16)

    def near(h, mid, low, high, *first):
        width = half if h == 0 else columns
        return call(
            functools.partial(near_kernel, size, h),
            (like((rows, width), BF16), flipped, own, term, term if h == 0 else long, term),
            [SMEM] * 3 + [VMEM] * (6 + len(first)),
            flops=2 * rows * half * (2 * columns + (slots - blocks) * size),
            moved=8 * rows * columns,
        )(core, y, result_mask.T, held, mid, low, high, slab, near_slab, *first)

    def send(part, step):
        return lax.ppermute(part, "y", ring(4, step))

    product0, flipped0, own0, up0, cross0, down0 = near(0, mid0, low0, high0)
    up0, down0 = send(up0, 1), send(down0, 3)
    product, flipped1, own1, up1, cross, down1 = near(1, mid1, low1, high1, product0, cross0)
    up1, down1, cross = send(up1, 1), send(down1, 3), send(cross, 2)
    far_slab = after(far_slab, own1, up0, down0)
    both_slab = lax.ppermute(far_slab, "core", swap)
    flipped1 = after(flipped1, up1, down1)
    far_own, far_up, far_cross, far_down = call(
        far_kernel,
        (long_own, long, long, long),
        [SMEM] * 2 + [VMEM] * 4,
        flops=8 * rows * half * columns,
        moved=8 * rows * columns,
    )(core, y, flipped0, flipped1, far_slab, both_slab)
    far_up, far_down, far_cross = send(far_up, 1), send(far_down, 3), send(far_cross, 2)
    deep = half // inner
    part = call(
        first_sum_kernel, like((2 * inner, deep, columns), BF16), [SMEM] + [VMEM] * 11, moved=8 * rows * half
    )(xh, own0, up0, down0, own1, up1, down1, cross, far_own, far_up, far_cross, far_down)
    part = lax.all_to_all(part, ("xl", "z"), 0, 0, tiled=True)
    factor = 1.0 / math.sqrt(rows * groups)
    projected = call(
        functools.partial(last_sum_kernel, factor), like((deep, columns), F32), [VMEM], moved=4 * deep * columns
    )(part)
    return (product, projected)


def solution(mesh):
    split = Mesh(mesh.devices.reshape(2, 2, 2, 4, 8), BLK + ROWS)
    placed = (P(ROWS, None), P(ROWS, None), P(ROWS, BLK), P(ROWS, BLK), P(ROWS, BLK))
    return jax.shard_map(
        on_device,
        mesh=split,
        in_specs=placed,
        out_specs=(P(ROWS, BLK), P(ROWS, BLK)),
        check_vma=False,
    )
```

```python
import functools
import math

import jax
import jax.numpy as jnp
from jax import lax
from jax.experimental import pallas as pl
from jax.experimental.pallas import tpu as pltpu
from jax.sharding import Mesh, PartitionSpec as P

F32, BF16 = jnp.float32, jnp.bfloat16
ROWS = ("xl", "y", "z")
BLK = ("xh", "core")
VMEM = pl.BlockSpec(memory_space=pltpu.VMEM)
SMEM = pl.BlockSpec(memory_space=pltpu.SMEM)
MIB = 1 << 20


def call(body, outs, ins, scratch=(), limit=8 * MIB, flops=0, moved=0):
    return pl.pallas_call(
        body,
        out_shape=outs,
        in_specs=ins,
        out_specs=jax.tree.map(lambda _: VMEM, outs),
        scratch_shapes=list(scratch),
        compiler_params=pltpu.CompilerParams(vmem_limit_bytes=limit),
        cost_estimate=pl.CostEstimate(flops=flops, bytes_accessed=moved, transcendentals=0),
    )


def dot(a, b):
    return jnp.dot(a, b, preferred_element_type=F32)


def mask_kernel(size, mask_ref, slab_hbm, h0_ref, h1_ref, both_ref, held, sems):
    panels, blocks = mask_ref.shape
    half = panels // 2
    copies = [
        pltpu.make_async_copy(slab_hbm.at[pl.ds(i * size, size)], held.at[i], sems.at[i])
        for i in range(blocks)
    ]
    for copy in copies:
        copy.start()
    for i, copy in enumerate(copies):
        copy.wait()
        rows = pl.ds(i * size, size)
        for j in range(panels):
            ref = (h0_ref, h1_ref)[j // half]
            tile = held[i, :, j * size : (j + 1) * size]
            tile = jnp.where(mask_ref[j, i] != 0, tile, jnp.zeros_like(tile))
            ref[rows, pl.ds((j % half) * size, size)] = tile
            both_ref[j // half, rows, pl.ds((j % half) * size, size)] = tile


def middle_kernel(size, fmask_ref, fock_ref, h0_ref, h1_ref, held_ref, m0_ref, m1_ref, token_ref):
    token_ref[...] = jnp.zeros_like(token_ref)
    blocks, slots = fmask_ref.shape
    for i in range(blocks):
        rows = pl.ds(i * size, size)
        for o in range(slots):
            cols = pl.ds(o * size, size)
            tile = fock_ref[rows, cols]
            held_ref[rows, cols] = jnp.where(fmask_ref[i, o] != 0, tile, jnp.zeros_like(tile))
        fock = held_ref[rows, pl.ds((blocks - i) * size, blocks * size)]
        m0_ref[rows, :] = dot(fock, h0_ref[...])
        m1_ref[rows, :] = dot(fock, h1_ref[...])


def pick_kernel(edge, own_ref, crossed_ref, up_ref, down_ref):
    y, z = lax.axis_index("y"), lax.axis_index("z")
    top, bottom = (y == edge[0] - 1) & (z == edge[1] - 1), (y == 0) & (z == 0)
    for ref, cross in ((up_ref, top), (down_ref, bottom)):

        @pl.when(cross)
        def _():
            ref[...] = crossed_ref[...]

        @pl.when(jnp.logical_not(cross))
        def _():
            ref[...] = own_ref[...]


def near_kernel(size, h, rmask_ref, held_ref, mid_ref, low_ref, high_ref, *rest):
    own_refs, near_ref, rest = rest[:2], rest[2], rest[3:]
    start = 0
    if h == 1:
        first_ref, rest = rest[0], rest[1:]
        start = first_ref.shape[1]
    out_ref, outt_ref, terms_ref = rest
    if h == 1:
        out_ref[:, :start] = first_ref[...]
    blocks = rmask_ref.shape[1]
    slots = held_ref.shape[1] // size
    panels = mid_ref.shape[1] // size
    for i in range(blocks):
        rows = pl.ds(i * size, size)
        total = mid_ref[rows, :]
        total += dot(held_ref[rows, : (blocks - i) * size], low_ref[i * size :, :])
        total += dot(held_ref[rows, (2 * blocks - i) * size :], high_ref[: (slots - 2 * blocks + i) * size, :])
        for j in range(panels):
            cols = slice(j * size, (j + 1) * size)
            tile = total[:, cols]
            keep = rmask_ref[h * panels + j, i] != 0
            tile = jnp.where(keep, tile, jnp.zeros_like(tile)).astype(BF16)
            out_ref[rows, pl.ds(start + j * size, size)] = tile
            outt_ref[cols, rows] = tile.T
    core = lax.axis_index("core")
    for k in range(2):
        terms_ref[core * 2 + k] = dot(outt_ref[...], own_refs[k][...]).astype(BF16)
        terms_ref[(1 - core) * 2 + k] = dot(outt_ref[...], near_ref[k]).astype(BF16)


def far_kernel(t0_ref, t1_ref, far_ref, terms_ref):
    half = t0_ref.shape[0]
    for c in range(2):
        for k, t in enumerate((t0_ref, t1_ref)):
            terms_ref[c, pl.ds(k * half, half), :] = dot(t[...], far_ref[c]).astype(BF16)


def gather_kernel(t0_ref, t1_ref, both_ref, near0_ref, near1_ref, far_ref, out_ref):
    half = t0_ref.shape[0]
    core, xh = lax.axis_index("core"), lax.axis_index("xh")
    other = (1 - xh) * 4
    for c in range(2):
        out_ref[other + core * 2 + c] = far_ref[c]
        for k, t in enumerate((t0_ref, t1_ref)):
            out_ref[other + (1 - core) * 2 + c, pl.ds(k * half, half), :] = dot(t[...], both_ref[c]).astype(BF16)
    for s in range(4):
        for k, ref in enumerate((near0_ref, near1_ref)):
            out_ref[xh * 4 + s, pl.ds(k * half, half), :] = ref[s]


def first_sum_kernel(in_ref, out_ref):
    total = in_ref[0].astype(F32)
    for s in range(1, in_ref.shape[0]):
        total += in_ref[s].astype(F32)
    out_ref[...] = total.T.astype(BF16)


def last_sum_kernel(factor, in_ref, out_ref):
    total = in_ref[0].astype(F32)
    for s in range(1, in_ref.shape[0]):
        total += in_ref[s].astype(F32)
    out_ref[...] = total * factor


def after(x, *others):
    anywhere = pl.BlockSpec(memory_space=pl.ANY)
    return pl.pallas_call(
        lambda *refs: None,
        out_shape=jax.ShapeDtypeStruct(x.shape, x.dtype),
        in_specs=[anywhere] * (1 + len(others)),
        out_specs=anywhere,
        input_output_aliases={0: 0},
        compiler_params=pltpu.CompilerParams(vmem_limit_bytes=MIB),
    )(x, *others)


def ring(count, step):
    return [(i, (i + step) % count) for i in range(count)]


def on_device(fock_band, fock_slot_mask, orbital_slab, orbital_mask, result_mask):
    blocks, slots = fock_slot_mask.shape
    rows, columns = orbital_slab.shape
    size = rows // blocks
    half = columns // 2
    like = jax.ShapeDtypeStruct
    groups, wide, deep = lax.axis_size(ROWS), lax.axis_size("y"), lax.axis_size("z")
    plane = wide * deep
    piece = like((rows, half), BF16)
    h0, h1, panels = call(
        functools.partial(mask_kernel, size),
        (piece, piece, like((2, rows, half), BF16)),
        [SMEM, pl.BlockSpec(memory_space=pltpu.HBM)],
        [pltpu.VMEM((blocks, size, columns), BF16), pltpu.SemaphoreType.DMA((blocks,))],
    )(orbital_mask.T, orbital_slab)
    swap = ring(2, 1)
    low0 = lax.ppermute(h0, ROWS, ring(groups, 1))
    high0 = lax.ppermute(h0, ROWS, ring(groups, groups - 1))
    ends = [(i, (i + plane) % groups) for i in range(groups) if i % plane in (0, plane - 1)]
    crossed = lax.ppermute(h1, ROWS, ends)
    far = lax.ppermute(panels, "xh", swap)
    near_panels = lax.ppermute(panels, "core", swap)
    held, mid0, mid1, token = call(
        functools.partial(middle_kernel, size),
        (like((rows, slots * size), BF16), *[like((rows, half), F32)] * 2, like((8, size), F32)),
        [SMEM, VMEM, VMEM, VMEM],
        flops=2 * rows * rows * columns,
        moved=4 * rows * slots * size,
    )(fock_slot_mask, fock_band, h0, h1)
    up1, down1 = call(
        functools.partial(pick_kernel, (wide, deep)), (piece, piece), [VMEM, VMEM], moved=8 * rows * half
    )(h1, after(crossed, low0, high0, token))
    within = [(i, i + 1 if (i + 1) % plane else i + 1 - plane) for i in range(groups)]
    low1 = lax.ppermute(up1, ROWS, within)
    high1 = lax.ppermute(down1, ROWS, [(b, a) for a, b in within])

    def near(h, mid, low, high, *first):
        width = half if h == 0 else columns
        return call(
            functools.partial(near_kernel, size, h),
            (like((rows, width), BF16), like((half, rows), BF16), like((4, half, half), BF16)),
            [SMEM] + [VMEM] * (7 + len(first)),
            flops=2 * rows * half * (2 * columns + (slots - blocks) * size),
            moved=8 * rows * columns,
        )(result_mask.T, held, mid, low, high, h0, h1, near_panels, *first)

    product0, flipped0, terms0 = near(0, mid0, low0, high0)
    product, flipped1, terms1 = near(1, mid1, low1, high1, product0)
    far = after(far, terms1)
    both = lax.ppermute(far, "core", swap)
    far_terms = call(
        far_kernel,
        like((2, columns, half), BF16),
        [VMEM] * 3,
        flops=4 * rows * half * columns,
        moved=8 * rows * half,
    )(flipped0, flipped1, far)
    terms = call(
        gather_kernel,
        like((groups // deep, columns, half), BF16),
        [VMEM] * 6,
        flops=4 * rows * half * columns,
        moved=8 * rows * columns,
    )(flipped0, flipped1, both, terms0, terms1, far_terms)
    terms = lax.all_to_all(terms, ("xl", "y"), 0, 0, tiled=True)
    part = call(first_sum_kernel, like((half, columns), BF16), [VMEM])(terms)
    part = part.reshape(deep, half // deep, columns)
    part = lax.all_to_all(part, "z", 0, 0, tiled=True)
    factor = 1.0 / math.sqrt(rows * groups)
    projected = call(
        functools.partial(last_sum_kernel, factor), like((half // deep, columns), F32), [VMEM]
    )(part)
    return (product, projected)


def solution(mesh):
    split = Mesh(mesh.devices.reshape(2, 2, 2, 4, 8), BLK + ROWS)
    placed = (P(ROWS, None), P(ROWS, None), P(ROWS, BLK), P(ROWS, BLK), P(ROWS, BLK))
    return jax.shard_map(
        on_device,
        mesh=split,
        in_specs=placed,
        out_specs=(P(ROWS, BLK), P(ROWS, BLK)),
        check_vma=False,
    )
```

```python
import functools
import math

import jax
import jax.numpy as jnp
from jax import lax
from jax.experimental import pallas as pl
from jax.experimental.pallas import tpu as pltpu
from jax.sharding import Mesh, PartitionSpec as P

F32, BF16 = jnp.float32, jnp.bfloat16
ROWS = ("xl", "y", "z")
BLK = ("xh", "core")
VMEM = pl.BlockSpec(memory_space=pltpu.VMEM)
SMEM = pl.BlockSpec(memory_space=pltpu.SMEM)
HBM = pl.BlockSpec(memory_space=pltpu.HBM)
MIB = 1 << 20


def call(body, outs, ins, scratch=(), limit=8 * MIB, flops=0, moved=0, place=VMEM):
    return pl.pallas_call(
        body,
        out_shape=outs,
        in_specs=ins,
        out_specs=jax.tree.map(lambda _: place, outs),
        scratch_shapes=list(scratch),
        compiler_params=pltpu.CompilerParams(vmem_limit_bytes=limit),
        cost_estimate=pl.CostEstimate(flops=flops, bytes_accessed=moved, transcendentals=0),
    )


def dot(a, b):
    return jnp.dot(a, b, preferred_element_type=F32)


def mask_kernel(size, mask_ref, slab_hbm, h0_hbm, h1_hbm, both_hbm, loaded, kept, in_sems, out_sems):
    panels, blocks = mask_ref.shape
    half = panels // 2
    at = [pl.ds(i * size, size) for i in range(blocks)]
    loads = [pltpu.make_async_copy(slab_hbm.at[at[i]], loaded.at[at[i]], in_sems.at[i]) for i in range(blocks)]
    for load in loads:
        load.start()
    stores = []
    for i, load in enumerate(loads):
        load.wait()
        for j in range(panels):
            tile = loaded[at[i], pl.ds(j * size, size)]
            tile = jnp.where(mask_ref[j, i] != 0, tile, jnp.zeros_like(tile))
            kept[j // half, at[i], pl.ds((j % half) * size, size)] = tile
        for h, ref in enumerate((h0_hbm, h1_hbm)):
            stores.append(pltpu.make_async_copy(kept.at[h, at[i]], ref.at[at[i]], out_sems.at[i, 2 * h]))
            stores.append(pltpu.make_async_copy(kept.at[h, at[i]], both_hbm.at[h, at[i]], out_sems.at[i, 2 * h + 1]))
        for store in stores[-4:]:
            store.start()
    for store in stores:
        store.wait()


def middle_kernel(size, fmask_ref, fock_ref, h0_ref, h1_ref, held_ref, m0_ref, m1_ref):
    blocks, slots = fmask_ref.shape
    for i in range(blocks):
        rows = pl.ds(i * size, size)
        for o in range(slots):
            cols = pl.ds(o * size, size)
            tile = fock_ref[rows, cols]
            held_ref[rows, cols] = jnp.where(fmask_ref[i, o] != 0, tile, jnp.zeros_like(tile))
        fock = held_ref[rows, pl.ds((blocks - i) * size, blocks * size)]
        m0_ref[rows, :] = dot(fock, h0_ref[...])
        m1_ref[rows, :] = dot(fock, h1_ref[...])


def pick_kernel(edge, own_ref, crossed_ref, up_ref, down_ref):
    y, z = lax.axis_index("y"), lax.axis_index("z")
    top, bottom = (y == edge[0] - 1) & (z == edge[1] - 1), (y == 0) & (z == 0)
    for ref, cross in ((up_ref, top), (down_ref, bottom)):

        @pl.when(cross)
        def _():
            ref[...] = crossed_ref[...]

        @pl.when(jnp.logical_not(cross))
        def _():
            ref[...] = own_ref[...]


def near_kernel(size, h, rmask_ref, held_ref, mid_ref, low_ref, high_ref, *rest):
    own_refs, near_ref, rest = rest[:2], rest[2], rest[3:]
    start = 0
    if h == 1:
        first_ref, rest = rest[0], rest[1:]
        start = first_ref.shape[1]
    out_ref, outt_ref, terms_ref = rest
    if h == 1:
        out_ref[:, :start] = first_ref[...]
    blocks = rmask_ref.shape[1]
    slots = held_ref.shape[1] // size
    panels = mid_ref.shape[1] // size
    for i in range(blocks):
        rows = pl.ds(i * size, size)
        total = mid_ref[rows, :]
        total += dot(held_ref[rows, : (blocks - i) * size], low_ref[i * size :, :])
        total += dot(held_ref[rows, (2 * blocks - i) * size :], high_ref[: (slots - 2 * blocks + i) * size, :])
        for j in range(panels):
            cols = slice(j * size, (j + 1) * size)
            tile = total[:, cols]
            keep = rmask_ref[h * panels + j, i] != 0
            tile = jnp.where(keep, tile, jnp.zeros_like(tile)).astype(BF16)
            out_ref[rows, pl.ds(start + j * size, size)] = tile
            outt_ref[cols, rows] = tile.T
    core = lax.axis_index("core")
    for k in range(2):
        terms_ref[core * 2 + k] = dot(outt_ref[...], own_refs[k][...]).astype(BF16)
        terms_ref[(1 - core) * 2 + k] = dot(outt_ref[...], near_ref[k]).astype(BF16)


def far_kernel(t0_ref, t1_ref, far_ref, terms_ref):
    half = t0_ref.shape[0]
    for c in range(2):
        for k, t in enumerate((t0_ref, t1_ref)):
            terms_ref[c, pl.ds(k * half, half), :] = dot(t[...], far_ref[c]).astype(BF16)


def gather_kernel(t0_ref, t1_ref, both_ref, near0_ref, near1_ref, far_ref, out_ref):
    half = t0_ref.shape[0]
    core, xh = lax.axis_index("core"), lax.axis_index("xh")
    other = (1 - xh) * 4
    for c in range(2):
        out_ref[other + core * 2 + c] = far_ref[c]
        for k, t in enumerate((t0_ref, t1_ref)):
            out_ref[other + (1 - core) * 2 + c, pl.ds(k * half, half), :] = dot(t[...], both_ref[c]).astype(BF16)
    for s in range(4):
        for k, ref in enumerate((near0_ref, near1_ref)):
            out_ref[xh * 4 + s, pl.ds(k * half, half), :] = ref[s]


def first_sum_kernel(in_ref, out_ref):
    total = in_ref[0].astype(F32)
    for s in range(1, in_ref.shape[0]):
        total += in_ref[s].astype(F32)
    out_ref[...] = total.T.astype(BF16)


def last_sum_kernel(factor, in_ref, out_ref):
    total = in_ref[0].astype(F32)
    for s in range(1, in_ref.shape[0]):
        total += in_ref[s].astype(F32)
    out_ref[...] = total * factor


def after(x, *others):
    anywhere = pl.BlockSpec(memory_space=pl.ANY)
    return pl.pallas_call(
        lambda *refs: None,
        out_shape=jax.ShapeDtypeStruct(x.shape, x.dtype),
        in_specs=[anywhere] * (1 + len(others)),
        out_specs=anywhere,
        input_output_aliases={0: 0},
        compiler_params=pltpu.CompilerParams(vmem_limit_bytes=MIB),
    )(x, *others)


def ring(count, step):
    return [(i, (i + step) % count) for i in range(count)]


def on_device(fock_band, fock_slot_mask, orbital_slab, orbital_mask, result_mask):
    blocks, slots = fock_slot_mask.shape
    rows, columns = orbital_slab.shape
    size = rows // blocks
    half = columns // 2
    like = jax.ShapeDtypeStruct
    groups, wide, deep = lax.axis_size(ROWS), lax.axis_size("y"), lax.axis_size("z")
    plane = wide * deep
    piece = like((rows, half), BF16)
    h0, h1, panels = call(
        functools.partial(mask_kernel, size),
        (piece, piece, like((2, rows, half), BF16)),
        [SMEM, HBM],
        [
            pltpu.VMEM((rows, columns), BF16),
            pltpu.VMEM((2, rows, half), BF16),
            pltpu.SemaphoreType.DMA((blocks,)),
            pltpu.SemaphoreType.DMA((blocks, 4)),
        ],
        limit=60 * MIB,
        place=HBM,
    )(orbital_mask.T, orbital_slab)
    swap = ring(2, 1)
    low0 = lax.ppermute(h0, ROWS, ring(groups, 1))
    high0 = lax.ppermute(h0, ROWS, ring(groups, groups - 1))
    ends = [(i, (i + plane) % groups) for i in range(groups) if i % plane in (0, plane - 1)]
    crossed = lax.ppermute(h1, ROWS, ends)
    far = lax.ppermute(panels, "xh", swap)
    near_panels = lax.ppermute(panels, "core", swap)
    held, mid0, mid1 = call(
        functools.partial(middle_kernel, size),
        (like((rows, slots * size), BF16), *[like((rows, half), F32)] * 2),
        [SMEM, VMEM, VMEM, VMEM],
        flops=2 * rows * rows * columns,
        moved=4 * rows * slots * size,
    )(fock_slot_mask, fock_band, h0, h1)
    up1, down1 = call(
        functools.partial(pick_kernel, (wide, deep)), (piece, piece), [VMEM, VMEM], moved=8 * rows * half
    )(h1, after(crossed, near_panels))
    within = [(i, i + 1 if (i + 1) % plane else i + 1 - plane) for i in range(groups)]
    low1 = lax.ppermute(up1, ROWS, within)
    high1 = lax.ppermute(down1, ROWS, [(b, a) for a, b in within])

    def near(h, mid, low, high, *first):
        width = half if h == 0 else columns
        return call(
            functools.partial(near_kernel, size, h),
            (like((rows, width), BF16), like((half, rows), BF16), like((4, half, half), BF16)),
            [SMEM] + [VMEM] * (7 + len(first)),
            flops=2 * rows * half * (2 * columns + (slots - blocks) * size),
            moved=8 * rows * columns,
        )(result_mask.T, held, mid, low, high, h0, h1, near_panels, *first)

    product0, flipped0, terms0 = near(0, mid0, low0, high0)
    product, flipped1, terms1 = near(1, mid1, low1, high1, product0)
    far = after(far, terms1)
    both = lax.ppermute(far, "core", swap)
    far_terms = call(
        far_kernel,
        like((2, columns, half), BF16),
        [VMEM] * 3,
        flops=4 * rows * half * columns,
        moved=8 * rows * half,
    )(flipped0, flipped1, far)
    terms = call(
        gather_kernel,
        like((groups // deep, columns, half), BF16),
        [VMEM] * 6,
        flops=4 * rows * half * columns,
        moved=8 * rows * columns,
    )(flipped0, flipped1, both, terms0, terms1, far_terms)
    terms = lax.all_to_all(terms, ("xl", "y"), 0, 0, tiled=True)
    part = call(first_sum_kernel, like((half, columns), BF16), [VMEM])(terms)
    part = part.reshape(deep, half // deep, columns)
    part = lax.all_to_all(part, "z", 0, 0, tiled=True)
    factor = 1.0 / math.sqrt(rows * groups)
    projected = call(
        functools.partial(last_sum_kernel, factor), like((half // deep, columns), F32), [VMEM]
    )(part)
    return (product, projected)


def solution(mesh):
    split = Mesh(mesh.devices.reshape(2, 2, 2, 4, 8), BLK + ROWS)
    placed = (P(ROWS, None), P(ROWS, None), P(ROWS, BLK), P(ROWS, BLK), P(ROWS, BLK))
    return jax.shard_map(
        on_device,
        mesh=split,
        in_specs=placed,
        out_specs=(P(ROWS, BLK), P(ROWS, BLK)),
        check_vma=False,
    )
```

```python
import functools
import math

import jax
import jax.numpy as jnp
from jax import lax
from jax.experimental import pallas as pl
from jax.experimental.pallas import tpu as pltpu
from jax.sharding import Mesh, PartitionSpec as P

F32, BF16 = jnp.float32, jnp.bfloat16
ROWS = ("xl", "y", "z")
BLK = ("xh", "core")
VMEM = pl.BlockSpec(memory_space=pltpu.VMEM)
SMEM = pl.BlockSpec(memory_space=pltpu.SMEM)
HBM = pl.BlockSpec(memory_space=pltpu.HBM)
MIB = 1 << 20


def call(body, outs, ins, scratch=(), limit=8 * MIB, flops=0, moved=0, place=VMEM):
    return pl.pallas_call(
        body,
        out_shape=outs,
        in_specs=ins,
        out_specs=jax.tree.map(lambda _: place, outs),
        scratch_shapes=list(scratch),
        compiler_params=pltpu.CompilerParams(vmem_limit_bytes=limit),
        cost_estimate=pl.CostEstimate(flops=flops, bytes_accessed=moved, transcendentals=0),
    )


def dot(a, b):
    return jnp.dot(a, b, preferred_element_type=F32)


def mask_kernel(size, mask_ref, slab_hbm, h0_hbm, h1_hbm, both_hbm, loaded, kept, in_sems, out_sems):
    panels, blocks = mask_ref.shape
    half = panels // 2
    at = [pl.ds(i * size, size) for i in range(blocks)]
    loads = [pltpu.make_async_copy(slab_hbm.at[at[i]], loaded.at[at[i]], in_sems.at[i]) for i in range(blocks)]
    for load in loads:
        load.start()
    stores = []
    for i, load in enumerate(loads):
        load.wait()
        for j in range(panels):
            tile = loaded[at[i], pl.ds(j * size, size)]
            tile = jnp.where(mask_ref[j, i] != 0, tile, jnp.zeros_like(tile))
            kept[j // half, at[i], pl.ds((j % half) * size, size)] = tile
        for h, ref in enumerate((h0_hbm, h1_hbm)):
            stores.append(pltpu.make_async_copy(kept.at[h, at[i]], ref.at[at[i]], out_sems.at[i, 2 * h]))
            stores.append(pltpu.make_async_copy(kept.at[h, at[i]], both_hbm.at[h, at[i]], out_sems.at[i, 2 * h + 1]))
        for store in stores[-4:]:
            store.start()
    for store in stores:
        store.wait()


def middle_kernel(size, fmask_ref, fock_ref, h0_ref, h1_ref, held_ref, m0_ref, m1_ref):
    blocks, slots = fmask_ref.shape
    for i in range(blocks):
        rows = pl.ds(i * size, size)
        for o in range(slots):
            cols = pl.ds(o * size, size)
            tile = fock_ref[rows, cols]
            held_ref[rows, cols] = jnp.where(fmask_ref[i, o] != 0, tile, jnp.zeros_like(tile))
        fock = held_ref[rows, pl.ds((blocks - i) * size, blocks * size)]
        m0_ref[rows, :] = dot(fock, h0_ref[...])
        m1_ref[rows, :] = dot(fock, h1_ref[...])


def pick_kernel(edge, own_ref, crossed_ref, up_ref, down_ref):
    y, z = lax.axis_index("y"), lax.axis_index("z")
    top, bottom = (y == edge[0] - 1) & (z == edge[1] - 1), (y == 0) & (z == 0)
    for ref, cross in ((up_ref, top), (down_ref, bottom)):

        @pl.when(cross)
        def _():
            ref[...] = crossed_ref[...]

        @pl.when(jnp.logical_not(cross))
        def _():
            ref[...] = own_ref[...]


def near_kernel(size, h, rmask_ref, held_ref, mid_ref, low_ref, high_ref, own0_ref, own1_ref, near_ref, *rest):
    start = 0
    if h == 1:
        (first_ref, *earlier), rest = rest[:5], rest[5:]
        start = first_ref.shape[1]
    out_ref, outt_ref, *to = rest
    if h == 1:
        out_ref[:, :start] = first_ref[...]
        for ref, part in zip(to, earlier):
            ref[:start, :] = part[...]
    blocks = rmask_ref.shape[1]
    slots = held_ref.shape[1] // size
    panels = mid_ref.shape[1] // size
    for i in range(blocks):
        rows = pl.ds(i * size, size)
        total = mid_ref[rows, :]
        total += dot(held_ref[rows, : (blocks - i) * size], low_ref[i * size :, :])
        total += dot(held_ref[rows, (2 * blocks - i) * size :], high_ref[: (slots - 2 * blocks + i) * size, :])
        for j in range(panels):
            cols = slice(j * size, (j + 1) * size)
            tile = total[:, cols]
            keep = rmask_ref[h * panels + j, i] != 0
            tile = jnp.where(keep, tile, jnp.zeros_like(tile)).astype(BF16)
            out_ref[rows, pl.ds(start + j * size, size)] = tile
            outt_ref[cols, rows] = tile.T
    project(outt_ref, ((own0_ref, own1_ref), (near_ref.at[0], near_ref.at[1])), [ref.at[pl.ds(start, outt_ref.shape[0]), :] for ref in to])


def project(outt_ref, panels, to):
    core, y = lax.axis_index("core"), lax.axis_index("y")
    for q, halves in enumerate(panels):
        for k, ref in enumerate(halves):
            terms = dot(outt_ref[...], ref[...])
            step = lax.rem((core ^ q) * 2 + k - y + 4, 4)
            for s, into in enumerate(to):

                @pl.when(step == s)
                def _():
                    into[...] = terms.astype(into.dtype)


def far_kernel(t0_ref, t1_ref, far_ref, both_ref, *to):
    half = t0_ref.shape[0]
    panels = [(ref.at[0], ref.at[1]) for ref in (far_ref, both_ref)]
    for k, t in enumerate((t0_ref, t1_ref)):
        project(t, panels, [ref.at[pl.ds(k * half, half), :] for ref in to])


def first_sum_kernel(*refs):
    out_ref = refs[-1]
    count, deep, _ = out_ref.shape
    inner = count // 2
    xh = lax.axis_index("xh")
    for f, parts in enumerate((refs[:4], refs[4:8])):
        total = parts[0][...]
        for part in parts[1:]:
            total += part[...].astype(F32)
        turned = total.T.astype(BF16)
        for z in range(inner):
            out_ref[(xh ^ f) * inner + z] = turned[z * deep : (z + 1) * deep]


def last_sum_kernel(factor, in_ref, out_ref):
    total = in_ref[0].astype(F32)
    for s in range(1, in_ref.shape[0]):
        total += in_ref[s].astype(F32)
    out_ref[...] = total * factor


def after(x, *others):
    anywhere = pl.BlockSpec(memory_space=pl.ANY)
    return pl.pallas_call(
        lambda *refs: None,
        out_shape=jax.ShapeDtypeStruct(x.shape, x.dtype),
        in_specs=[anywhere] * (1 + len(others)),
        out_specs=anywhere,
        input_output_aliases={0: 0},
        compiler_params=pltpu.CompilerParams(vmem_limit_bytes=MIB),
    )(x, *others)


def ring(count, step):
    return [(i, (i + step) % count) for i in range(count)]


def on_device(fock_band, fock_slot_mask, orbital_slab, orbital_mask, result_mask):
    blocks, slots = fock_slot_mask.shape
    rows, columns = orbital_slab.shape
    size = rows // blocks
    half = columns // 2
    like = jax.ShapeDtypeStruct
    groups, wide, deep = lax.axis_size(ROWS), lax.axis_size("y"), lax.axis_size("z")
    plane = wide * deep
    piece = like((rows, half), BF16)
    h0, h1, panels = call(
        functools.partial(mask_kernel, size),
        (piece, piece, like((2, rows, half), BF16)),
        [SMEM, HBM],
        [
            pltpu.VMEM((rows, columns), BF16),
            pltpu.VMEM((2, rows, half), BF16),
            pltpu.SemaphoreType.DMA((blocks,)),
            pltpu.SemaphoreType.DMA((blocks, 4)),
        ],
        limit=60 * MIB,
        place=HBM,
    )(orbital_mask.T, orbital_slab)
    swap = ring(2, 1)
    low0 = lax.ppermute(h0, ROWS, ring(groups, 1))
    high0 = lax.ppermute(h0, ROWS, ring(groups, groups - 1))
    ends = [(i, (i + plane) % groups) for i in range(groups) if i % plane in (0, plane - 1)]
    crossed = lax.ppermute(h1, ROWS, ends)
    far = lax.ppermute(panels, "xh", swap)
    near_panels = lax.ppermute(panels, "core", swap)
    held, mid0, mid1 = call(
        functools.partial(middle_kernel, size),
        (like((rows, slots * size), BF16), *[like((rows, half), F32)] * 2),
        [SMEM, VMEM, VMEM, VMEM],
        flops=2 * rows * rows * columns,
        moved=4 * rows * slots * size,
    )(fock_slot_mask, fock_band, h0, h1)
    up1, down1 = call(
        functools.partial(pick_kernel, (wide, deep)), (piece, piece), [VMEM, VMEM], moved=8 * rows * half
    )(h1, after(crossed, near_panels))
    within = [(i, i + 1 if (i + 1) % plane else i + 1 - plane) for i in range(groups)]
    low1 = lax.ppermute(up1, ROWS, within)
    high1 = lax.ppermute(down1, ROWS, [(b, a) for a, b in within])

    own, long = like((columns, half), F32), like((columns, half), BF16)
    square = [like((half, half), kind) for kind in (F32, BF16, BF16, BF16)]

    def near(h, mid, low, high, *first):
        return call(
            functools.partial(near_kernel, size, h),
            (like((rows, half * (h + 1)), BF16), like((half, rows), BF16), *(square, (own, long, long, long))[h]),
            [SMEM] + [VMEM] * (7 + len(first)),
            flops=2 * rows * half * (2 * columns + (slots - blocks) * size),
            moved=8 * rows * columns,
        )(result_mask.T, held, mid, low, high, h0, h1, near_panels, *first)

    def send(*parts):
        return [lax.ppermute(part, "y", ring(wide, s + 1)) for s, part in enumerate(parts)]

    product0, flipped0, *parts = near(0, mid0, low0, high0)
    product, flipped1, near_own, *parts = near(1, mid1, low1, high1, product0, *parts)
    near_got = send(*parts)
    far = after(far, *near_got)
    both = lax.ppermute(far, "core", swap)
    far_own, *parts = call(
        far_kernel,
        (own, long, long, long),
        [VMEM] * 4,
        flops=8 * rows * half * columns,
        moved=8 * rows * columns,
    )(flipped0, flipped1, far, both)
    far_got = send(*parts)
    part = call(first_sum_kernel, like((2 * deep, half // deep, columns), BF16), [VMEM] * 8, moved=8 * rows * half)(
        near_own, *near_got, far_own, *far_got
    )
    part = lax.all_to_all(part, ("xl", "z"), 0, 0, tiled=True)
    factor = 1.0 / math.sqrt(rows * groups)
    projected = call(
        functools.partial(last_sum_kernel, factor), like((half // deep, columns), F32), [VMEM]
    )(part)
    return (product, projected)


def solution(mesh):
    split = Mesh(mesh.devices.reshape(2, 2, 2, 4, 8), BLK + ROWS)
    placed = (P(ROWS, None), P(ROWS, None), P(ROWS, BLK), P(ROWS, BLK), P(ROWS, BLK))
    return jax.shard_map(
        on_device,
        mesh=split,
        in_specs=placed,
        out_specs=(P(ROWS, BLK), P(ROWS, BLK)),
        check_vma=False,
    )
```

```python
import functools
import math

import jax
import jax.numpy as jnp
from jax import lax
from jax.experimental import pallas as pl
from jax.experimental.pallas import tpu as pltpu
from jax.sharding import Mesh, PartitionSpec as P

F32, BF16 = jnp.float32, jnp.bfloat16
ROWS = ("xl", "y", "z")
BLK = ("xh", "core")
VMEM = pl.BlockSpec(memory_space=pltpu.VMEM)
SMEM = pl.BlockSpec(memory_space=pltpu.SMEM)
HBM = pl.BlockSpec(memory_space=pltpu.HBM)
MIB = 1 << 20


def call(body, outs, ins, scratch=(), limit=8 * MIB, flops=0, moved=0, place=VMEM):
    return pl.pallas_call(
        body,
        out_shape=outs,
        in_specs=ins,
        out_specs=jax.tree.map(lambda _: place, outs),
        scratch_shapes=list(scratch),
        compiler_params=pltpu.CompilerParams(vmem_limit_bytes=limit),
        cost_estimate=pl.CostEstimate(flops=flops, bytes_accessed=moved, transcendentals=0),
    )


def dot(a, b):
    return jnp.dot(a, b, preferred_element_type=F32)


def mask_kernel(size, mask_ref, slab_hbm, out_hbm, held, in_sems, out_sems):
    panels, blocks = mask_ref.shape
    at = [pl.ds(i * size, size) for i in range(blocks)]
    loads = [pltpu.make_async_copy(slab_hbm.at[at[i]], held.at[at[i]], in_sems.at[i]) for i in range(blocks)]
    stores = [pltpu.make_async_copy(held.at[at[i]], out_hbm.at[at[i]], out_sems.at[i]) for i in range(blocks)]
    for load in loads:
        load.start()
    for i in range(blocks):
        loads[i].wait()
        for j in range(panels):
            cols = pl.ds(j * size, size)
            tile = held[at[i], cols]
            held[at[i], cols] = jnp.where(mask_ref[j, i] != 0, tile, jnp.zeros_like(tile))
        stores[i].start()
    for store in stores:
        store.wait()


def middle_kernel(size, fmask_ref, fock_ref, slab_ref, held_ref, mid_ref, again_ref):
    again_ref[...] = slab_ref[...]
    blocks, slots = fmask_ref.shape
    for i in range(blocks):
        rows = pl.ds(i * size, size)
        for o in range(slots):
            cols = pl.ds(o * size, size)
            tile = fock_ref[rows, cols]
            held_ref[rows, cols] = jnp.where(fmask_ref[i, o] != 0, tile, jnp.zeros_like(tile))
        mid_ref[rows, :] = dot(held_ref[rows, pl.ds((blocks - i) * size, blocks * size)], slab_ref[...])


def near_kernel(size, rmask_ref, held_ref, mid_ref, low_ref, high_ref, own_ref, near_ref, out_ref, outt_ref, *to):
    panels, blocks = rmask_ref.shape
    slots = held_ref.shape[1] // size
    for i in range(blocks):
        rows = pl.ds(i * size, size)
        total = mid_ref[rows, :]
        total += dot(held_ref[rows, : (blocks - i) * size], low_ref[i * size :, :])
        total += dot(held_ref[rows, (2 * blocks - i) * size :], high_ref[: (slots - 2 * blocks + i) * size, :])
        for j in range(panels):
            cols = slice(j * size, (j + 1) * size)
            tile = total[:, cols]
            tile = jnp.where(rmask_ref[j, i] != 0, tile, jnp.zeros_like(tile)).astype(BF16)
            out_ref[rows, cols] = tile
            outt_ref[cols, rows] = tile.T
    half = to[0].shape[1]
    for q, ref in enumerate((own_ref, near_ref)):
        for k in range(2):
            project(outt_ref, ref[:, pl.ds(k * half, half)], q, k, enumerate(to))


def project(outt_ref, panel, q, k, to):
    terms = dot(outt_ref[...], panel)
    step = lax.rem((lax.axis_index("core") ^ q) * 2 + k - lax.axis_index("y") + 4, 4)
    for s, into in to:

        @pl.when(step == s)
        def _():
            into[...] = terms.astype(into.dtype)


def merge_kernel(edge, early_hbm, late_hbm, out_hbm, sem):
    y, z = lax.axis_index("y"), lax.axis_index("z")

    @pl.when(crossing(edge, y, z))
    def _():
        copy = pltpu.make_async_copy(late_hbm, out_hbm, sem)
        copy.start()
        copy.wait()


def crossing(edge, y, z):
    return ((y == edge[0] - 1) & (z == 0)) | ((y == 0) & (z == edge[1] - 1))


def far_kernel(outt_ref, far_ref, both_ref, *to):
    half = to[0].shape[1]
    for q, ref in enumerate((far_ref, both_ref)):
        for k in range(2):
            project(outt_ref, ref[:, pl.ds(k * half, half)], q, k, enumerate(to))


def first_sum_kernel(*refs):
    out_ref = refs[-1]
    count, deep, _ = out_ref.shape
    inner = count // 2
    xh = lax.axis_index("xh")
    for f, parts in enumerate((refs[:4], refs[4:8])):
        total = parts[0][...]
        for part in parts[1:]:
            total += part[...].astype(F32)
        turned = total.T.astype(BF16)
        for z in range(inner):
            out_ref[(xh ^ f) * inner + z] = turned[z * deep : (z + 1) * deep]


def last_sum_kernel(factor, in_ref, out_ref):
    total = in_ref[0].astype(F32)
    for s in range(1, in_ref.shape[0]):
        total += in_ref[s].astype(F32)
    out_ref[...] = total * factor


def after(x, *others):
    anywhere = pl.BlockSpec(memory_space=pl.ANY)
    return pl.pallas_call(
        lambda *refs: None,
        out_shape=jax.ShapeDtypeStruct(x.shape, x.dtype),
        in_specs=[anywhere] * (1 + len(others)),
        out_specs=anywhere,
        input_output_aliases={0: 0},
        compiler_params=pltpu.CompilerParams(vmem_limit_bytes=MIB),
    )(x, *others)


def ring(count, step):
    return [(i, (i + step) % count) for i in range(count)]


def on_device(fock_band, fock_slot_mask, orbital_slab, orbital_mask, result_mask):
    blocks, slots = fock_slot_mask.shape
    rows, columns = orbital_slab.shape
    size = rows // blocks
    half = columns // 2
    like = jax.ShapeDtypeStruct
    groups, wide, deep = lax.axis_size(ROWS), lax.axis_size("y"), lax.axis_size("z")
    whole = like((rows, columns), BF16)
    slab = call(
        functools.partial(mask_kernel, size),
        whole,
        [SMEM, HBM],
        [pltpu.VMEM((rows, columns), BF16), *[pltpu.SemaphoreType.DMA((blocks,))] * 2],
        limit=60 * MIB,
        place=HBM,
    )(orbital_mask.T, orbital_slab)
    swap = ring(2, 1)
    low = lax.ppermute(slab, ROWS, ring(groups, 1))
    high = lax.ppermute(slab, ROWS, ring(groups, groups - 1))
    near_slab = lax.ppermute(slab, "core", swap)
    edge = (wide, deep)
    pairs = [], []
    for i in range(2 * groups):
        late = crossing(edge, i // deep % wide, i % deep)
        pairs[late].append((i, (i + groups) % (2 * groups)))
    early_far = lax.ppermute(slab, ("xh", *ROWS), pairs[0])
    held, mid, again = call(
        functools.partial(middle_kernel, size),
        (like((rows, slots * size), BF16), like((rows, columns), F32), whole),
        [SMEM, VMEM, VMEM],
        flops=2 * rows * rows * columns,
        moved=4 * rows * slots * size,
    )(fock_slot_mask, fock_band, slab)
    late_far = lax.ppermute(after(again, low, high, early_far), ("xh", *ROWS), pairs[1])
    own, long = like((columns, half), F32), like((columns, half), BF16)
    product, flipped, near_own, *parts = call(
        functools.partial(near_kernel, size),
        (whole, like((columns, rows), BF16), own, long, long, long),
        [SMEM] + [VMEM] * 6,
        flops=2 * rows * columns * (2 * columns + (slots - blocks) * size),
        moved=16 * rows * columns,
        limit=16 * MIB,
    )(result_mask.T, held, mid, low, high, slab, near_slab)

    def send(part, step):
        return lax.ppermute(part, "y", ring(wide, step))

    near_got = [send(part, step + 1) for step, part in enumerate(parts)]

    anywhere = pl.BlockSpec(memory_space=pl.ANY)
    far = pl.pallas_call(
        functools.partial(merge_kernel, edge),
        out_shape=whole,
        in_specs=[anywhere] * 2,
        out_specs=anywhere,
        scratch_shapes=[pltpu.SemaphoreType.DMA],
        input_output_aliases={0: 0},
        compiler_params=pltpu.CompilerParams(vmem_limit_bytes=MIB),
    )(early_far, after(late_far, *near_got))
    both = lax.ppermute(far, "core", swap)
    far_own, *parts = call(
        far_kernel,
        (own, long, long, long),
        [VMEM] * 3,
        flops=4 * rows * columns * columns,
        moved=16 * rows * half,
    )(flipped, far, both)
    far_got = [send(part, step + 1) for step, part in enumerate(parts)]
    part = call(first_sum_kernel, like((2 * deep, half // deep, columns), BF16), [VMEM] * 8, moved=8 * rows * half)(
        near_own, *near_got, far_own, *far_got
    )
    part = lax.all_to_all(part, ("xl", "z"), 0, 0, tiled=True)
    factor = 1.0 / math.sqrt(rows * groups)
    projected = call(
        functools.partial(last_sum_kernel, factor), like((half // deep, columns), F32), [VMEM]
    )(part)
    return (product, projected)


def solution(mesh):
    split = Mesh(mesh.devices.reshape(2, 2, 2, 4, 8), BLK + ROWS)
    placed = (P(ROWS, None), P(ROWS, None), P(ROWS, BLK), P(ROWS, BLK), P(ROWS, BLK))
    return jax.shard_map(
        on_device,
        mesh=split,
        in_specs=placed,
        out_specs=(P(ROWS, BLK), P(ROWS, BLK)),
        check_vma=False,
    )
```

```python
import functools
import math

import jax
import jax.numpy as jnp
from jax import lax
from jax.experimental import pallas as pl
from jax.experimental.pallas import tpu as pltpu
from jax.sharding import Mesh, PartitionSpec as P

F32, BF16 = jnp.float32, jnp.bfloat16
ROWS = ("xl", "y", "z")
BLK = ("xh", "core")
VMEM = pl.BlockSpec(memory_space=pltpu.VMEM)
SMEM = pl.BlockSpec(memory_space=pltpu.SMEM)
HBM = pl.BlockSpec(memory_space=pltpu.HBM)
MIB = 1 << 20


def call(body, outs, ins, scratch=(), limit=8 * MIB, flops=0, moved=0, place=VMEM):
    return pl.pallas_call(
        body,
        out_shape=outs,
        in_specs=ins,
        out_specs=jax.tree.map(lambda _: place, outs),
        scratch_shapes=list(scratch),
        compiler_params=pltpu.CompilerParams(vmem_limit_bytes=limit),
        cost_estimate=pl.CostEstimate(flops=flops, bytes_accessed=moved, transcendentals=0),
    )


def dot(a, b):
    return jnp.dot(a, b, preferred_element_type=F32)


def mask_kernel(size, mask_ref, slab_hbm, out_hbm, top_hbm, low_hbm, held, in_sems, out_sems):
    panels, blocks = mask_ref.shape
    at = [pl.ds(i * size, size) for i in range(blocks)]
    loads = [pltpu.make_async_copy(slab_hbm.at[at[i]], held.at[at[i]], in_sems.at[i]) for i in range(blocks)]
    stores = []
    for load in loads:
        load.start()
    for i in range(blocks):
        loads[i].wait()
        for j in range(panels):
            cols = pl.ds(j * size, size)
            tile = held[at[i], cols]
            held[at[i], cols] = jnp.where(mask_ref[j, i] != 0, tile, jnp.zeros_like(tile))
        part = (top_hbm, low_hbm)[i // (blocks // 2)].at[at[i % (blocks // 2)]]
        for k, to in enumerate((out_hbm.at[at[i]], part)):
            stores.append(pltpu.make_async_copy(held.at[at[i]], to, out_sems.at[i, k]))
            stores[-1].start()
    for store in stores:
        store.wait()


def middle_kernel(size, fmask_ref, fock_ref, slab_ref, held_ref, mid_ref):
    blocks, slots = fmask_ref.shape
    for i in range(blocks):
        rows = pl.ds(i * size, size)
        for o in range(slots):
            cols = pl.ds(o * size, size)
            tile = fock_ref[rows, cols]
            held_ref[rows, cols] = jnp.where(fmask_ref[i, o] != 0, tile, jnp.zeros_like(tile))
        mid_ref[rows, :] = dot(held_ref[rows, pl.ds((blocks - i) * size, blocks * size)], slab_ref[...])


def product_kernel(size, rmask_ref, held_ref, mid_ref, low_ref, high_ref, out_ref, outt_ref):
    panels, blocks = rmask_ref.shape
    slots = held_ref.shape[1] // size
    for i in range(blocks):
        rows = pl.ds(i * size, size)
        total = mid_ref[rows, :]
        total += dot(held_ref[rows, : (blocks - i) * size], low_ref[i * size :, :])
        total += dot(held_ref[rows, (2 * blocks - i) * size :], high_ref[: (slots - 2 * blocks + i) * size, :])
        for j in range(panels):
            cols = slice(j * size, (j + 1) * size)
            tile = total[:, cols]
            tile = jnp.where(rmask_ref[j, i] != 0, tile, jnp.zeros_like(tile)).astype(BF16)
            out_ref[rows, cols] = tile
            outt_ref[cols, rows] = tile.T


def merge_kernel(edge, direct_hbm, top_hbm, low_hbm, out_hbm, sems):
    @pl.when(crossing(edge, lax.axis_index("y"), lax.axis_index("z")))
    def _():
        count = top_hbm.shape[0]
        copies = [
            pltpu.make_async_copy(part, out_hbm.at[pl.ds(k * count, count)], sems.at[k])
            for k, part in enumerate((top_hbm, low_hbm))
        ]
        for copy in copies:
            copy.start()
        for copy in copies:
            copy.wait()


def crossing(edge, y, z):
    return ((y == edge[0] - 1) & (z == 0)) | ((y == 0) & (z == edge[1] - 1))


def terms_kernel(flipped_ref, *refs):
    *panel_refs, out_ref = refs
    half = out_ref.shape[2]
    core = lax.axis_index("core")
    for q, ref in enumerate(panel_refs):
        for k in range(2):
            terms = dot(flipped_ref[...], ref[:, pl.ds(k * half, half)]).astype(BF16)
            at = k if len(panel_refs) == 1 else (core ^ q) * 2 + k
            out_ref[at] = terms


def gather_kernel(flipped_ref, both_ref, near_ref, far_ref, out_ref):
    half = out_ref.shape[2]
    core, xh = lax.axis_index("core"), lax.axis_index("xh")
    other = (1 - xh) * 4
    for k in range(2):
        terms = dot(flipped_ref[...], both_ref[:, pl.ds(k * half, half)])
        out_ref[other + (1 - core) * 2 + k] = terms.astype(BF16)
        out_ref[other + core * 2 + k] = far_ref[k]
    for s in range(4):
        out_ref[xh * 4 + s] = near_ref[s]


def first_sum_kernel(in_ref, out_ref):
    total = in_ref[0].astype(F32)
    for s in range(1, in_ref.shape[0]):
        total += in_ref[s].astype(F32)
    out_ref[...] = total.T.astype(BF16)


def last_sum_kernel(factor, in_ref, out_ref):
    total = in_ref[0].astype(F32)
    for s in range(1, in_ref.shape[0]):
        total += in_ref[s].astype(F32)
    out_ref[...] = total * factor


def after(x, *others):
    anywhere = pl.BlockSpec(memory_space=pl.ANY)
    return pl.pallas_call(
        lambda *refs: None,
        out_shape=jax.ShapeDtypeStruct(x.shape, x.dtype),
        in_specs=[anywhere] * (1 + len(others)),
        out_specs=anywhere,
        input_output_aliases={0: 0},
        compiler_params=pltpu.CompilerParams(vmem_limit_bytes=MIB),
    )(x, *others)


def ring(count, step):
    return [(i, (i + step) % count) for i in range(count)]


def on_device(fock_band, fock_slot_mask, orbital_slab, orbital_mask, result_mask):
    blocks, slots = fock_slot_mask.shape
    rows, columns = orbital_slab.shape
    size = rows // blocks
    half = columns // 2
    like = jax.ShapeDtypeStruct
    groups, wide, deep = lax.axis_size(ROWS), lax.axis_size("y"), lax.axis_size("z")
    whole, part = like((rows, columns), BF16), like((rows // 2, columns), BF16)
    slab, top, bottom = call(
        functools.partial(mask_kernel, size),
        (whole, part, part),
        [SMEM, HBM],
        [
            pltpu.VMEM((rows, columns), BF16),
            pltpu.SemaphoreType.DMA((blocks,)),
            pltpu.SemaphoreType.DMA((blocks, 2)),
        ],
        limit=60 * MIB,
        place=HBM,
    )(orbital_mask.T, orbital_slab)
    swap = ring(2, 1)
    low = lax.ppermute(slab, ROWS, ring(groups, 1))
    high = lax.ppermute(slab, ROWS, ring(groups, groups - 1))
    near_slab = lax.ppermute(slab, "core", swap)
    edge = (wide, deep)
    every = ("xh", *ROWS)
    direct, out, back = [], ([], []), ([], [])
    for i in range(2 * groups):
        partner = (i + groups) % (2 * groups)
        y, z = i // deep % wide, i % deep
        if not crossing(edge, y, z):
            direct.append((i, partner))
            continue
        for k, shift in enumerate((1, wide - 1)):
            relay = i + ((y + shift) % wide - y) * deep
            out[k].append((i, relay))
            back[k].append((relay, partner))
    far = lax.ppermute(slab, every, direct)
    sent = [lax.ppermute(x, every, pairs) for x, pairs in zip((top, bottom), out)]
    late = [lax.ppermute(x, every, pairs) for x, pairs in zip(sent, back)]
    held, mid = call(
        functools.partial(middle_kernel, size),
        (like((rows, slots * size), BF16), like((rows, columns), F32)),
        [SMEM, VMEM, VMEM],
        flops=2 * rows * rows * columns,
        moved=4 * rows * slots * size,
    )(fock_slot_mask, fock_band, slab)
    product, flipped = call(
        functools.partial(product_kernel, size),
        (whole, like((columns, rows), BF16)),
        [SMEM] + [VMEM] * 4,
        flops=2 * rows * columns * (slots - blocks) * size,
        moved=16 * rows * columns,
    )(result_mask.T, held, mid, low, high)
    anywhere = pl.BlockSpec(memory_space=pl.ANY)
    far = pl.pallas_call(
        functools.partial(merge_kernel, edge),
        out_shape=whole,
        in_specs=[anywhere] * 3,
        out_specs=anywhere,
        scratch_shapes=[pltpu.SemaphoreType.DMA((2,))],
        input_output_aliases={0: 0},
        compiler_params=pltpu.CompilerParams(vmem_limit_bytes=MIB),
    )(far, late[0], after(late[1], flipped))
    both = lax.ppermute(far, "core", swap)

    def terms(count, *panels):
        return call(
            terms_kernel,
            like((count, columns, half), BF16),
            [VMEM] * (1 + len(panels)),
            flops=2 * rows * columns * count * half,
            moved=2 * rows * columns * 4,
        )(flipped, *panels)

    pieces = call(
        gather_kernel,
        like((8, columns, half), BF16),
        [VMEM] * 4,
        flops=2 * rows * columns * columns,
        moved=8 * rows * columns,
    )(flipped, both, terms(4, slab, near_slab), terms(2, far))
    pieces = lax.all_to_all(pieces, ("xl", "y"), 0, 0, tiled=True)
    part = call(first_sum_kernel, like((half, columns), BF16), [VMEM])(pieces)
    part = part.reshape(deep, half // deep, columns)
    part = lax.all_to_all(part, "z", 0, 0, tiled=True)
    factor = 1.0 / math.sqrt(rows * groups)
    projected = call(
        functools.partial(last_sum_kernel, factor), like((half // deep, columns), F32), [VMEM]
    )(part)
    return (product, projected)


def solution(mesh):
    split = Mesh(mesh.devices.reshape(2, 2, 2, 4, 8), BLK + ROWS)
    placed = (P(ROWS, None), P(ROWS, None), P(ROWS, BLK), P(ROWS, BLK), P(ROWS, BLK))
    return jax.shard_map(
        on_device,
        mesh=split,
        in_specs=placed,
        out_specs=(P(ROWS, BLK), P(ROWS, BLK)),
        check_vma=False,
    )
```

```python
import functools
import math

import jax
import jax.numpy as jnp
from jax import lax
from jax.experimental import pallas as pl
from jax.experimental.pallas import tpu as pltpu
from jax.sharding import Mesh, PartitionSpec as P

F32, BF16 = jnp.float32, jnp.bfloat16
ROWS = ("xl", "y", "z")
BLK = ("xh", "core")
VMEM = pl.BlockSpec(memory_space=pltpu.VMEM)
SMEM = pl.BlockSpec(memory_space=pltpu.SMEM)
HBM = pl.BlockSpec(memory_space=pltpu.HBM)
MIB = 1 << 20


def call(body, outs, ins, scratch=(), limit=8 * MIB, flops=0, moved=0, place=VMEM):
    return pl.pallas_call(
        body,
        out_shape=outs,
        in_specs=ins,
        out_specs=jax.tree.map(lambda _: place, outs),
        scratch_shapes=list(scratch),
        compiler_params=pltpu.CompilerParams(vmem_limit_bytes=limit),
        cost_estimate=pl.CostEstimate(flops=flops, bytes_accessed=moved, transcendentals=0),
    )


def dot(a, b):
    return jnp.dot(a, b, preferred_element_type=F32)


def mask_kernel(size, mask_ref, slab_hbm, h0_hbm, h1_hbm, both_hbm, loaded, kept, in_sems, out_sems):
    panels, blocks = mask_ref.shape
    half = panels // 2
    at = [pl.ds(i * size, size) for i in range(blocks)]
    loads = [pltpu.make_async_copy(slab_hbm.at[at[i]], loaded.at[at[i]], in_sems.at[i]) for i in range(blocks)]
    for load in loads:
        load.start()
    stores = []
    for i, load in enumerate(loads):
        load.wait()
        for j in range(panels):
            tile = loaded[at[i], pl.ds(j * size, size)]
            tile = jnp.where(mask_ref[j, i] != 0, tile, jnp.zeros_like(tile))
            kept[j // half, at[i], pl.ds((j % half) * size, size)] = tile
        for h, ref in enumerate((h0_hbm, h1_hbm)):
            stores.append(pltpu.make_async_copy(kept.at[h, at[i]], ref.at[at[i]], out_sems.at[i, 2 * h]))
            stores.append(pltpu.make_async_copy(kept.at[h, at[i]], both_hbm.at[h, at[i]], out_sems.at[i, 2 * h + 1]))
        for store in stores[-4:]:
            store.start()
    for store in stores:
        store.wait()


def middle_kernel(size, fmask_ref, fock_ref, h0_ref, h1_ref, held_ref, m0_ref, m1_ref):
    blocks, slots = fmask_ref.shape
    for i in range(blocks):
        rows = pl.ds(i * size, size)
        for o in range(slots):
            cols = pl.ds(o * size, size)
            tile = fock_ref[rows, cols]
            held_ref[rows, cols] = jnp.where(fmask_ref[i, o] != 0, tile, jnp.zeros_like(tile))
        fock = held_ref[rows, pl.ds((blocks - i) * size, blocks * size)]
        m0_ref[rows, :] = dot(fock, h0_ref[...])
        m1_ref[rows, :] = dot(fock, h1_ref[...])


def pick_kernel(edge, own_ref, crossed_ref, up_ref, down_ref):
    y, z = lax.axis_index("y"), lax.axis_index("z")
    top, bottom = (y == edge[0] - 1) & (z == edge[1] - 1), (y == 0) & (z == 0)
    for ref, cross in ((up_ref, top), (down_ref, bottom)):

        @pl.when(cross)
        def _():
            ref[...] = crossed_ref[...]

        @pl.when(jnp.logical_not(cross))
        def _():
            ref[...] = own_ref[...]


def near_kernel(size, h, rmask_ref, held_ref, mid_ref, low_ref, high_ref, *rest):
    own_refs, near_ref, rest = rest[:2], rest[2], rest[3:]
    start = 0
    if h == 1:
        first_ref, rest = rest[0], rest[1:]
        start = first_ref.shape[1]
    out_ref, outt_ref, terms_ref = rest
    if h == 1:
        out_ref[:, :start] = first_ref[...]
    blocks = rmask_ref.shape[1]
    slots = held_ref.shape[1] // size
    panels = mid_ref.shape[1] // size
    for i in range(blocks):
        rows = pl.ds(i * size, size)
        total = mid_ref[rows, :]
        total += dot(held_ref[rows, : (blocks - i) * size], low_ref[i * size :, :])
        total += dot(held_ref[rows, (2 * blocks - i) * size :], high_ref[: (slots - 2 * blocks + i) * size, :])
        for j in range(panels):
            cols = slice(j * size, (j + 1) * size)
            tile = total[:, cols]
            keep = rmask_ref[h * panels + j, i] != 0
            tile = jnp.where(keep, tile, jnp.zeros_like(tile)).astype(BF16)
            out_ref[rows, pl.ds(start + j * size, size)] = tile
            outt_ref[cols, rows] = tile.T
    core = lax.axis_index("core")
    for k in range(2):
        terms_ref[core * 2 + k] = dot(outt_ref[...], own_refs[k][...]).astype(BF16)
        terms_ref[(1 - core) * 2 + k] = dot(outt_ref[...], near_ref[k]).astype(BF16)


def far_kernel(t0_ref, t1_ref, far_ref, terms_ref):
    half = t0_ref.shape[0]
    for c in range(2):
        for k, t in enumerate((t0_ref, t1_ref)):
            terms_ref[c, pl.ds(k * half, half), :] = dot(t[...], far_ref[c]).astype(BF16)


def gather_kernel(t0_ref, t1_ref, both_ref, near0_ref, near1_ref, far_ref, *refs):
    *out_refs, held = refs
    half = t0_ref.shape[0]
    core, xh, xl, y = (lax.axis_index(name) for name in ("core", "xh", "xl", "y"))
    for c in range(2):
        held[core * 2 + c] = far_ref[c]
        for k, t in enumerate((t0_ref, t1_ref)):
            held[(1 - core) * 2 + c, pl.ds(k * half, half), :] = dot(t[...], both_ref[c]).astype(BF16)
    count = len(out_refs) // 2
    for near_here in (True, False):

        @pl.when((xh == xl) == near_here)
        def _():
            for s in range(count):
                to = lax.rem(y + s, count)
                near, far = (out_refs[s], out_refs[count + s])[:: 1 if near_here else -1]
                for k, ref in enumerate((near0_ref, near1_ref)):
                    near[pl.ds(k * half, half), :] = ref[to]
                far[...] = held[to]


def first_sum_kernel(*refs):
    *in_refs, out_ref = refs
    total = in_refs[0][...].astype(F32)
    for ref in in_refs[1:]:
        total += ref[...].astype(F32)
    out_ref[...] = total.T.astype(BF16)


def last_sum_kernel(factor, in_ref, out_ref):
    total = in_ref[0].astype(F32)
    for s in range(1, in_ref.shape[0]):
        total += in_ref[s].astype(F32)
    out_ref[...] = total * factor


def after(x, *others):
    anywhere = pl.BlockSpec(memory_space=pl.ANY)
    return pl.pallas_call(
        lambda *refs: None,
        out_shape=jax.ShapeDtypeStruct(x.shape, x.dtype),
        in_specs=[anywhere] * (1 + len(others)),
        out_specs=anywhere,
        input_output_aliases={0: 0},
        compiler_params=pltpu.CompilerParams(vmem_limit_bytes=MIB),
    )(x, *others)


def ring(count, step):
    return [(i, (i + step) % count) for i in range(count)]


def on_device(fock_band, fock_slot_mask, orbital_slab, orbital_mask, result_mask):
    blocks, slots = fock_slot_mask.shape
    rows, columns = orbital_slab.shape
    size = rows // blocks
    half = columns // 2
    like = jax.ShapeDtypeStruct
    groups, wide, deep = lax.axis_size(ROWS), lax.axis_size("y"), lax.axis_size("z")
    plane = wide * deep
    piece = like((rows, half), BF16)
    h0, h1, panels = call(
        functools.partial(mask_kernel, size),
        (piece, piece, like((2, rows, half), BF16)),
        [SMEM, HBM],
        [
            pltpu.VMEM((rows, columns), BF16),
            pltpu.VMEM((2, rows, half), BF16),
            pltpu.SemaphoreType.DMA((blocks,)),
            pltpu.SemaphoreType.DMA((blocks, 4)),
        ],
        limit=60 * MIB,
        place=HBM,
    )(orbital_mask.T, orbital_slab)
    swap = ring(2, 1)
    low0 = lax.ppermute(h0, ROWS, ring(groups, 1))
    high0 = lax.ppermute(h0, ROWS, ring(groups, groups - 1))
    ends = [(i, (i + plane) % groups) for i in range(groups) if i % plane in (0, plane - 1)]
    crossed = lax.ppermute(h1, ROWS, ends)
    far = lax.ppermute(panels, "xh", swap)
    near_panels = lax.ppermute(panels, "core", swap)
    held, mid0, mid1 = call(
        functools.partial(middle_kernel, size),
        (like((rows, slots * size), BF16), *[like((rows, half), F32)] * 2),
        [SMEM, VMEM, VMEM, VMEM],
        flops=2 * rows * rows * columns,
        moved=4 * rows * slots * size,
    )(fock_slot_mask, fock_band, h0, h1)
    up1, down1 = call(
        functools.partial(pick_kernel, (wide, deep)), (piece, piece), [VMEM, VMEM], moved=8 * rows * half
    )(h1, after(crossed, near_panels))
    within = [(i, i + 1 if (i + 1) % plane else i + 1 - plane) for i in range(groups)]
    low1 = lax.ppermute(up1, ROWS, within)
    high1 = lax.ppermute(down1, ROWS, [(b, a) for a, b in within])

    def near(h, mid, low, high, *first):
        width = half if h == 0 else columns
        return call(
            functools.partial(near_kernel, size, h),
            (like((rows, width), BF16), like((half, rows), BF16), like((4, half, half), BF16)),
            [SMEM] + [VMEM] * (7 + len(first)),
            flops=2 * rows * half * (2 * columns + (slots - blocks) * size),
            moved=8 * rows * columns,
        )(result_mask.T, held, mid, low, high, h0, h1, near_panels, *first)

    product0, flipped0, terms0 = near(0, mid0, low0, high0)
    product, flipped1, terms1 = near(1, mid1, low1, high1, product0)
    far = after(far, terms1)
    both = lax.ppermute(far, "core", swap)
    far_terms = call(
        far_kernel,
        like((2, columns, half), BF16),
        [VMEM] * 3,
        flops=4 * rows * half * columns,
        moved=8 * rows * half,
    )(flipped0, flipped1, far)
    piece = like((columns, half), BF16)
    pieces = list(call(
        gather_kernel,
        [piece] * (2 * wide),
        [VMEM] * 6,
        [pltpu.VMEM((wide, columns, half), BF16)],
        flops=4 * rows * half * columns,
        moved=8 * rows * columns,
    )(flipped0, flipped1, both, terms0, terms1, far_terms))
    for step in range(1, 2 * wide):
        across, along = divmod(step, wide)
        pairs = [(x * wide + y, (x ^ across) * wide + (y + along) % wide) for x in range(2) for y in range(wide)]
        pieces[step] = lax.ppermute(pieces[step], ("xl", "y"), pairs)
    part = call(first_sum_kernel, like((half, columns), BF16), [VMEM] * (2 * wide), limit=12 * MIB)(*pieces)
    part = part.reshape(deep, half // deep, columns)
    part = lax.all_to_all(part, "z", 0, 0, tiled=True)
    factor = 1.0 / math.sqrt(rows * groups)
    projected = call(
        functools.partial(last_sum_kernel, factor), like((half // deep, columns), F32), [VMEM]
    )(part)
    return (product, projected)


def solution(mesh):
    split = Mesh(mesh.devices.reshape(2, 2, 2, 4, 8), BLK + ROWS)
    placed = (P(ROWS, None), P(ROWS, None), P(ROWS, BLK), P(ROWS, BLK), P(ROWS, BLK))
    return jax.shard_map(
        on_device,
        mesh=split,
        in_specs=placed,
        out_specs=(P(ROWS, BLK), P(ROWS, BLK)),
        check_vma=False,
    )
```

```python
import functools
import math

import jax
import jax.numpy as jnp
from jax import lax
from jax.experimental import pallas as pl
from jax.experimental.pallas import tpu as pltpu
from jax.sharding import Mesh, PartitionSpec as P

F32, BF16 = jnp.float32, jnp.bfloat16
ROWS = ("xl", "y", "z")
BLK = ("xh", "core")
VMEM = pl.BlockSpec(memory_space=pltpu.VMEM)
SMEM = pl.BlockSpec(memory_space=pltpu.SMEM)
HBM = pl.BlockSpec(memory_space=pltpu.HBM)
MIB = 1 << 20


def call(body, outs, ins, scratch=(), limit=8 * MIB, flops=0, moved=0, place=VMEM):
    return pl.pallas_call(
        body,
        out_shape=outs,
        in_specs=ins,
        out_specs=jax.tree.map(lambda _: place, outs),
        scratch_shapes=list(scratch),
        compiler_params=pltpu.CompilerParams(vmem_limit_bytes=limit),
        cost_estimate=pl.CostEstimate(flops=flops, bytes_accessed=moved, transcendentals=0),
    )


def dot(a, b):
    return jnp.dot(a, b, preferred_element_type=F32)


def mask_kernel(size, mask_ref, slab_hbm, h0_hbm, h1_hbm, both_hbm, loaded, kept, in_sems, out_sems):
    panels, blocks = mask_ref.shape
    half = panels // 2
    at = [pl.ds(i * size, size) for i in range(blocks)]
    loads = [pltpu.make_async_copy(slab_hbm.at[at[i]], loaded.at[at[i]], in_sems.at[i]) for i in range(blocks)]
    for load in loads:
        load.start()
    stores = []
    for i, load in enumerate(loads):
        load.wait()
        for j in range(panels):
            tile = loaded[at[i], pl.ds(j * size, size)]
            tile = jnp.where(mask_ref[j, i] != 0, tile, jnp.zeros_like(tile))
            kept[j // half, at[i], pl.ds((j % half) * size, size)] = tile
        for h, ref in enumerate((h0_hbm, h1_hbm)):
            stores.append(pltpu.make_async_copy(kept.at[h, at[i]], ref.at[at[i]], out_sems.at[i, 2 * h]))
            stores.append(pltpu.make_async_copy(kept.at[h, at[i]], both_hbm.at[h, at[i]], out_sems.at[i, 2 * h + 1]))
        for store in stores[-4:]:
            store.start()
    for store in stores:
        store.wait()


def middle_kernel(size, fmask_ref, fock_ref, h0_ref, h1_ref, held_ref, m0_ref, m1_ref):
    blocks, slots = fmask_ref.shape
    for i in range(blocks):
        rows = pl.ds(i * size, size)
        for o in range(slots):
            cols = pl.ds(o * size, size)
            tile = fock_ref[rows, cols]
            held_ref[rows, cols] = jnp.where(fmask_ref[i, o] != 0, tile, jnp.zeros_like(tile))
        fock = held_ref[rows, pl.ds((blocks - i) * size, blocks * size)]
        m0_ref[rows, :] = dot(fock, h0_ref[...])
        m1_ref[rows, :] = dot(fock, h1_ref[...])


def pick_kernel(edge, own_ref, crossed_ref, up_ref, down_ref):
    y, z = lax.axis_index("y"), lax.axis_index("z")
    top, bottom = (y == edge[0] - 1) & (z == edge[1] - 1), (y == 0) & (z == 0)
    for ref, cross in ((up_ref, top), (down_ref, bottom)):

        @pl.when(cross)
        def _():
            ref[...] = crossed_ref[...]

        @pl.when(jnp.logical_not(cross))
        def _():
            ref[...] = own_ref[...]


def near_kernel(size, h, rmask_ref, held_ref, mid_ref, low_ref, high_ref, *rest):
    own_refs, near_ref, rest = rest[:2], rest[2], rest[3:]
    start = 0
    if h == 1:
        first_ref, earlier_ref, rest = rest[0], rest[1], rest[2:]
        start = first_ref.shape[1]
    out_ref, outt_ref, terms_ref = rest
    if h == 1:
        out_ref[:, :start] = first_ref[...]
        terms_ref[:, :start, :] = earlier_ref[...]
    blocks = rmask_ref.shape[1]
    slots = held_ref.shape[1] // size
    panels = mid_ref.shape[1] // size
    for i in range(blocks):
        rows = pl.ds(i * size, size)
        total = mid_ref[rows, :]
        total += dot(held_ref[rows, : (blocks - i) * size], low_ref[i * size :, :])
        total += dot(held_ref[rows, (2 * blocks - i) * size :], high_ref[: (slots - 2 * blocks + i) * size, :])
        for j in range(panels):
            cols = slice(j * size, (j + 1) * size)
            tile = total[:, cols]
            keep = rmask_ref[h * panels + j, i] != 0
            tile = jnp.where(keep, tile, jnp.zeros_like(tile)).astype(BF16)
            out_ref[rows, pl.ds(start + j * size, size)] = tile
            outt_ref[cols, rows] = tile.T
    core, deep = lax.axis_index("core"), pl.ds(start, outt_ref.shape[0])
    for k in range(2):
        terms_ref[core * 2 + k, deep, :] = dot(outt_ref[...], own_refs[k][...]).astype(BF16)
        terms_ref[(1 - core) * 2 + k, deep, :] = dot(outt_ref[...], near_ref[k]).astype(BF16)


def far_kernel(t0_ref, t1_ref, far_ref, terms_ref):
    half = t0_ref.shape[0]
    for c in range(2):
        for k, t in enumerate((t0_ref, t1_ref)):
            terms_ref[c, pl.ds(k * half, half), :] = dot(t[...], far_ref[c]).astype(BF16)


def gather_kernel(t0_ref, t1_ref, both_ref, far_ref, out_ref):
    half = t0_ref.shape[0]
    core = lax.axis_index("core")
    for c in range(2):
        out_ref[core * 2 + c] = far_ref[c]
        for k, t in enumerate((t0_ref, t1_ref)):
            out_ref[(1 - core) * 2 + c, pl.ds(k * half, half), :] = dot(t[...], both_ref[c]).astype(BF16)


def first_sum_kernel(near_ref, far_ref, out_ref):
    count, deep, _ = out_ref.shape
    inner = count // 2
    xh = lax.axis_index("xh")
    for f, ref in enumerate((near_ref, far_ref)):
        total = ref[0].astype(F32)
        for s in range(1, ref.shape[0]):
            total += ref[s].astype(F32)
        turned = total.T.astype(BF16)
        for z in range(inner):
            out_ref[(xh ^ f) * inner + z] = turned[z * deep : (z + 1) * deep]


def last_sum_kernel(factor, in_ref, out_ref):
    total = in_ref[0].astype(F32)
    for s in range(1, in_ref.shape[0]):
        total += in_ref[s].astype(F32)
    out_ref[...] = total * factor


def after(x, *others):
    anywhere = pl.BlockSpec(memory_space=pl.ANY)
    return pl.pallas_call(
        lambda *refs: None,
        out_shape=jax.ShapeDtypeStruct(x.shape, x.dtype),
        in_specs=[anywhere] * (1 + len(others)),
        out_specs=anywhere,
        input_output_aliases={0: 0},
        compiler_params=pltpu.CompilerParams(vmem_limit_bytes=MIB),
    )(x, *others)


def ring(count, step):
    return [(i, (i + step) % count) for i in range(count)]


def on_device(fock_band, fock_slot_mask, orbital_slab, orbital_mask, result_mask):
    blocks, slots = fock_slot_mask.shape
    rows, columns = orbital_slab.shape
    size = rows // blocks
    half = columns // 2
    like = jax.ShapeDtypeStruct
    groups, wide, deep = lax.axis_size(ROWS), lax.axis_size("y"), lax.axis_size("z")
    plane = wide * deep
    piece = like((rows, half), BF16)
    h0, h1, panels = call(
        functools.partial(mask_kernel, size),
        (piece, piece, like((2, rows, half), BF16)),
        [SMEM, HBM],
        [
            pltpu.VMEM((rows, columns), BF16),
            pltpu.VMEM((2, rows, half), BF16),
            pltpu.SemaphoreType.DMA((blocks,)),
            pltpu.SemaphoreType.DMA((blocks, 4)),
        ],
        limit=60 * MIB,
        place=HBM,
    )(orbital_mask.T, orbital_slab)
    swap = ring(2, 1)
    low0 = lax.ppermute(h0, ROWS, ring(groups, 1))
    high0 = lax.ppermute(h0, ROWS, ring(groups, groups - 1))
    ends = [(i, (i + plane) % groups) for i in range(groups) if i % plane in (0, plane - 1)]
    crossed = lax.ppermute(h1, ROWS, ends)
    far = lax.ppermute(panels, "xh", swap)
    near_panels = lax.ppermute(panels, "core", swap)
    held, mid0, mid1 = call(
        functools.partial(middle_kernel, size),
        (like((rows, slots * size), BF16), *[like((rows, half), F32)] * 2),
        [SMEM, VMEM, VMEM, VMEM],
        flops=2 * rows * rows * columns,
        moved=4 * rows * slots * size,
    )(fock_slot_mask, fock_band, h0, h1)
    up1, down1 = call(
        functools.partial(pick_kernel, (wide, deep)), (piece, piece), [VMEM, VMEM], moved=8 * rows * half
    )(h1, after(crossed, near_panels))
    within = [(i, i + 1 if (i + 1) % plane else i + 1 - plane) for i in range(groups)]
    low1 = lax.ppermute(up1, ROWS, within)
    high1 = lax.ppermute(down1, ROWS, [(b, a) for a, b in within])

    def near(h, mid, low, high, *first):
        width = half if h == 0 else columns
        return call(
            functools.partial(near_kernel, size, h),
            (like((rows, width), BF16), like((half, rows), BF16), like((wide, width, half), BF16)),
            [SMEM] + [VMEM] * (7 + len(first)),
            flops=2 * rows * half * (2 * columns + (slots - blocks) * size),
            moved=8 * rows * columns,
        )(result_mask.T, held, mid, low, high, h0, h1, near_panels, *first)

    product0, flipped0, terms0 = near(0, mid0, low0, high0)
    product, flipped1, terms1 = near(1, mid1, low1, high1, product0, terms0)
    near_got = lax.all_to_all(terms1, "y", 0, 0, tiled=True)
    far = after(far, terms1)
    both = lax.ppermute(far, "core", swap)
    far_terms = call(
        far_kernel,
        like((2, columns, half), BF16),
        [VMEM] * 3,
        flops=4 * rows * half * columns,
        moved=8 * rows * half,
    )(flipped0, flipped1, far)
    terms = call(
        gather_kernel,
        like((wide, columns, half), BF16),
        [VMEM] * 4,
        flops=4 * rows * half * columns,
        moved=8 * rows * columns,
    )(flipped0, flipped1, both, far_terms)
    far_got = lax.all_to_all(terms, "y", 0, 0, tiled=True)
    part = call(first_sum_kernel, like((2 * deep, half // deep, columns), BF16), [VMEM] * 2)(near_got, far_got)
    part = lax.all_to_all(part, ("xl", "z"), 0, 0, tiled=True)
    factor = 1.0 / math.sqrt(rows * groups)
    projected = call(
        functools.partial(last_sum_kernel, factor), like((half // deep, columns), F32), [VMEM]
    )(part)
    return (product, projected)


def solution(mesh):
    split = Mesh(mesh.devices.reshape(2, 2, 2, 4, 8), BLK + ROWS)
    placed = (P(ROWS, None), P(ROWS, None), P(ROWS, BLK), P(ROWS, BLK), P(ROWS, BLK))
    return jax.shard_map(
        on_device,
        mesh=split,
        in_specs=placed,
        out_specs=(P(ROWS, BLK), P(ROWS, BLK)),
        check_vma=False,
    )
```

```python
import functools
import math

import jax
import jax.numpy as jnp
from jax import lax
from jax.experimental import pallas as pl
from jax.experimental.pallas import tpu as pltpu
from jax.sharding import Mesh, PartitionSpec as P

F32, BF16 = jnp.float32, jnp.bfloat16
ROWS = ("xl", "y", "z")
BLK = ("xh", "core")
VMEM = pl.BlockSpec(memory_space=pltpu.VMEM)
SMEM = pl.BlockSpec(memory_space=pltpu.SMEM)
HBM = pl.BlockSpec(memory_space=pltpu.HBM)
MIB = 1 << 20


def call(body, outs, ins, scratch=(), limit=8 * MIB, flops=0, moved=0, place=VMEM):
    return pl.pallas_call(
        body,
        out_shape=outs,
        in_specs=ins,
        out_specs=jax.tree.map(lambda _: place, outs),
        scratch_shapes=list(scratch),
        compiler_params=pltpu.CompilerParams(vmem_limit_bytes=limit),
        cost_estimate=pl.CostEstimate(flops=flops, bytes_accessed=moved, transcendentals=0),
    )


def dot(a, b):
    return jnp.dot(a, b, preferred_element_type=F32)


def mask_kernel(size, mask_ref, slab_hbm, h0_hbm, h1_hbm, both_hbm, loaded, kept, in_sems, out_sems):
    panels, blocks = mask_ref.shape
    half = panels // 2
    at = [pl.ds(i * size, size) for i in range(blocks)]
    loads = [pltpu.make_async_copy(slab_hbm.at[at[i]], loaded.at[at[i]], in_sems.at[i]) for i in range(blocks)]
    for load in loads:
        load.start()
    stores = []
    for i, load in enumerate(loads):
        load.wait()
        for j in range(panels):
            tile = loaded[at[i], pl.ds(j * size, size)]
            tile = jnp.where(mask_ref[j, i] != 0, tile, jnp.zeros_like(tile))
            kept[j // half, at[i], pl.ds((j % half) * size, size)] = tile
        for h, ref in enumerate((h0_hbm, h1_hbm)):
            stores.append(pltpu.make_async_copy(kept.at[h, at[i]], ref.at[at[i]], out_sems.at[i, 2 * h]))
            stores.append(pltpu.make_async_copy(kept.at[h, at[i]], both_hbm.at[h, at[i]], out_sems.at[i, 2 * h + 1]))
        for store in stores[-4:]:
            store.start()
    for store in stores:
        store.wait()


def middle_kernel(size, fmask_ref, fock_ref, h0_ref, h1_ref, held_ref, m0_ref, m1_ref):
    blocks, slots = fmask_ref.shape
    for i in range(blocks):
        rows = pl.ds(i * size, size)
        for o in range(slots):
            cols = pl.ds(o * size, size)
            tile = fock_ref[rows, cols]
            held_ref[rows, cols] = jnp.where(fmask_ref[i, o] != 0, tile, jnp.zeros_like(tile))
        fock = held_ref[rows, pl.ds((blocks - i) * size, blocks * size)]
        m0_ref[rows, :] = dot(fock, h0_ref[...])
        m1_ref[rows, :] = dot(fock, h1_ref[...])


def pick_kernel(edge, own_ref, crossed_ref, up_ref, down_ref):
    y, z = lax.axis_index("y"), lax.axis_index("z")
    top, bottom = (y == edge[0] - 1) & (z == edge[1] - 1), (y == 0) & (z == 0)
    for ref, cross in ((up_ref, top), (down_ref, bottom)):

        @pl.when(cross)
        def _():
            ref[...] = crossed_ref[...]

        @pl.when(jnp.logical_not(cross))
        def _():
            ref[...] = own_ref[...]


def near_kernel(size, h, rmask_ref, held_ref, mid_ref, low_ref, high_ref, *rest):
    own_refs, near_ref, rest = rest[:2], rest[2], rest[3:]
    start = 0
    if h == 1:
        first_ref, rest = rest[0], rest[1:]
        start = first_ref.shape[1]
    out_ref, outt_ref, terms_ref = rest
    if h == 1:
        out_ref[:, :start] = first_ref[...]
    blocks = rmask_ref.shape[1]
    slots = held_ref.shape[1] // size
    panels = mid_ref.shape[1] // size
    for i in range(blocks):
        rows = pl.ds(i * size, size)
        total = mid_ref[rows, :]
        total += dot(held_ref[rows, : (blocks - i) * size], low_ref[i * size :, :])
        total += dot(held_ref[rows, (2 * blocks - i) * size :], high_ref[: (slots - 2 * blocks + i) * size, :])
        for j in range(panels):
            cols = slice(j * size, (j + 1) * size)
            tile = total[:, cols]
            keep = rmask_ref[h * panels + j, i] != 0
            tile = jnp.where(keep, tile, jnp.zeros_like(tile)).astype(BF16)
            out_ref[rows, pl.ds(start + j * size, size)] = tile
            outt_ref[cols, rows] = tile.T
    core = lax.axis_index("core")
    for k in range(2):
        terms_ref[core * 2 + k] = dot(outt_ref[...], own_refs[k][...]).astype(BF16)
        terms_ref[(1 - core) * 2 + k] = dot(outt_ref[...], near_ref[k]).astype(BF16)


def far_kernel(t0_ref, t1_ref, far_ref, terms_ref):
    half = t0_ref.shape[0]
    for c in range(2):
        for k, t in enumerate((t0_ref, t1_ref)):
            terms_ref[c, :, pl.ds(k * half, half)] = dot(t[...], far_ref[c]).astype(BF16)


def gather_kernel(t0_ref, t1_ref, both_ref, near0_ref, near1_ref, far_ref, out_ref):
    half = t0_ref.shape[0]
    core, xh = lax.axis_index("core"), lax.axis_index("xh")
    other = (1 - xh) * 4
    for c in range(2):
        out_ref[other + core * 2 + c] = far_ref[c]
        for k, t in enumerate((t0_ref, t1_ref)):
            out_ref[other + (1 - core) * 2 + c, :, pl.ds(k * half, half)] = dot(t[...], both_ref[c]).astype(BF16)
    for s in range(4):
        for k, ref in enumerate((near0_ref, near1_ref)):
            out_ref[xh * 4 + s, :, pl.ds(k * half, half)] = ref[s]


def first_sum_kernel(in_ref, out_ref):
    total = in_ref[0].astype(F32)
    for s in range(1, in_ref.shape[0]):
        total += in_ref[s].astype(F32)
    half = total.shape[0]
    for k in range(2):
        out_ref[:, pl.ds(k * half, half)] = total[:, k * half : (k + 1) * half].T.astype(BF16)


def last_sum_kernel(factor, in_ref, out_ref):
    total = in_ref[0].astype(F32)
    for s in range(1, in_ref.shape[0]):
        total += in_ref[s].astype(F32)
    out_ref[...] = total * factor


def after(x, *others):
    anywhere = pl.BlockSpec(memory_space=pl.ANY)
    return pl.pallas_call(
        lambda *refs: None,
        out_shape=jax.ShapeDtypeStruct(x.shape, x.dtype),
        in_specs=[anywhere] * (1 + len(others)),
        out_specs=anywhere,
        input_output_aliases={0: 0},
        compiler_params=pltpu.CompilerParams(vmem_limit_bytes=MIB),
    )(x, *others)


def ring(count, step):
    return [(i, (i + step) % count) for i in range(count)]


def on_device(fock_band, fock_slot_mask, orbital_slab, orbital_mask, result_mask):
    blocks, slots = fock_slot_mask.shape
    rows, columns = orbital_slab.shape
    size = rows // blocks
    half = columns // 2
    like = jax.ShapeDtypeStruct
    groups, wide, deep = lax.axis_size(ROWS), lax.axis_size("y"), lax.axis_size("z")
    plane = wide * deep
    piece = like((rows, half), BF16)
    h0, h1, panels = call(
        functools.partial(mask_kernel, size),
        (piece, piece, like((2, rows, half), BF16)),
        [SMEM, HBM],
        [
            pltpu.VMEM((rows, columns), BF16),
            pltpu.VMEM((2, rows, half), BF16),
            pltpu.SemaphoreType.DMA((blocks,)),
            pltpu.SemaphoreType.DMA((blocks, 4)),
        ],
        limit=60 * MIB,
        place=HBM,
    )(orbital_mask.T, orbital_slab)
    swap = ring(2, 1)
    low0 = lax.ppermute(h0, ROWS, ring(groups, 1))
    high0 = lax.ppermute(h0, ROWS, ring(groups, groups - 1))
    ends = [(i, (i + plane) % groups) for i in range(groups) if i % plane in (0, plane - 1)]
    crossed = lax.ppermute(h1, ROWS, ends)
    far = lax.ppermute(panels, "xh", swap)
    near_panels = lax.ppermute(panels, "core", swap)
    held, mid0, mid1 = call(
        functools.partial(middle_kernel, size),
        (like((rows, slots * size), BF16), *[like((rows, half), F32)] * 2),
        [SMEM, VMEM, VMEM, VMEM],
        flops=2 * rows * rows * columns,
        moved=4 * rows * slots * size,
    )(fock_slot_mask, fock_band, h0, h1)
    up1, down1 = call(
        functools.partial(pick_kernel, (wide, deep)), (piece, piece), [VMEM, VMEM], moved=8 * rows * half
    )(h1, after(crossed, near_panels))
    within = [(i, i + 1 if (i + 1) % plane else i + 1 - plane) for i in range(groups)]
    low1 = lax.ppermute(up1, ROWS, within)
    high1 = lax.ppermute(down1, ROWS, [(b, a) for a, b in within])

    def near(h, mid, low, high, *first):
        width = half if h == 0 else columns
        return call(
            functools.partial(near_kernel, size, h),
            (like((rows, width), BF16), like((half, rows), BF16), like((4, half, half), BF16)),
            [SMEM] + [VMEM] * (7 + len(first)),
            flops=2 * rows * half * (2 * columns + (slots - blocks) * size),
            moved=8 * rows * columns,
        )(result_mask.T, held, mid, low, high, h0, h1, near_panels, *first)

    product0, flipped0, terms0 = near(0, mid0, low0, high0)
    product, flipped1, terms1 = near(1, mid1, low1, high1, product0)
    far = after(far, terms1)
    both = lax.ppermute(far, "core", swap)
    far_terms = call(
        far_kernel,
        like((2, half, columns), BF16),
        [VMEM] * 3,
        flops=4 * rows * half * columns,
        moved=8 * rows * half,
    )(flipped0, flipped1, far)
    terms = call(
        gather_kernel,
        like((groups // deep, half, columns), BF16),
        [VMEM] * 6,
        flops=4 * rows * half * columns,
        moved=8 * rows * columns,
    )(flipped0, flipped1, both, terms0, terms1, far_terms)
    terms = lax.all_to_all(terms, ("xl", "y"), 0, 0, tiled=True)
    part = call(first_sum_kernel, like((half, columns), BF16), [VMEM])(terms)
    part = part.reshape(deep, half // deep, columns)
    part = lax.all_to_all(part, "z", 0, 0, tiled=True)
    factor = 1.0 / math.sqrt(rows * groups)
    projected = call(
        functools.partial(last_sum_kernel, factor), like((half // deep, columns), F32), [VMEM]
    )(part)
    return (product, projected)


def solution(mesh):
    split = Mesh(mesh.devices.reshape(2, 2, 2, 4, 8), BLK + ROWS)
    placed = (P(ROWS, None), P(ROWS, None), P(ROWS, BLK), P(ROWS, BLK), P(ROWS, BLK))
    return jax.shard_map(
        on_device,
        mesh=split,
        in_specs=placed,
        out_specs=(P(ROWS, BLK), P(ROWS, BLK)),
        check_vma=False,
    )
```

```python
import functools
import math

import jax
import jax.numpy as jnp
from jax import lax
from jax.experimental import pallas as pl
from jax.experimental.pallas import tpu as pltpu
from jax.sharding import Mesh, PartitionSpec as P

F32, BF16 = jnp.float32, jnp.bfloat16
ROWS = ("xl", "y", "z")
BLK = ("xh", "core")
VMEM = pl.BlockSpec(memory_space=pltpu.VMEM)
SMEM = pl.BlockSpec(memory_space=pltpu.SMEM)
HBM = pl.BlockSpec(memory_space=pltpu.HBM)
MIB = 1 << 20


def call(body, outs, ins, scratch=(), limit=8 * MIB, flops=0, moved=0, place=VMEM):
    return pl.pallas_call(
        body,
        out_shape=outs,
        in_specs=ins,
        out_specs=jax.tree.map(lambda _: place, outs),
        scratch_shapes=list(scratch),
        compiler_params=pltpu.CompilerParams(vmem_limit_bytes=limit),
        cost_estimate=pl.CostEstimate(flops=flops, bytes_accessed=moved, transcendentals=0),
    )


def dot(a, b):
    return jnp.dot(a, b, preferred_element_type=F32)


def mask_kernel(size, mask_ref, slab_hbm, h0_hbm, h1_hbm, both_hbm, loaded, kept, in_sems, out_sems):
    panels, blocks = mask_ref.shape
    half = panels // 2
    at = [pl.ds(i * size, size) for i in range(blocks)]
    loads = [pltpu.make_async_copy(slab_hbm.at[at[i]], loaded.at[at[i]], in_sems.at[i]) for i in range(blocks)]
    for load in loads:
        load.start()
    stores = []
    for i, load in enumerate(loads):
        load.wait()
        for j in range(panels):
            tile = loaded[at[i], pl.ds(j * size, size)]
            tile = jnp.where(mask_ref[j, i] != 0, tile, jnp.zeros_like(tile))
            kept[j // half, at[i], pl.ds((j % half) * size, size)] = tile
        for h, ref in enumerate((h0_hbm, h1_hbm)):
            stores.append(pltpu.make_async_copy(kept.at[h, at[i]], ref.at[at[i]], out_sems.at[i, 2 * h]))
            stores.append(pltpu.make_async_copy(kept.at[h, at[i]], both_hbm.at[h, at[i]], out_sems.at[i, 2 * h + 1]))
        for store in stores[-4:]:
            store.start()
    for store in stores:
        store.wait()


def middle_kernel(size, fmask_ref, fock_ref, h0_ref, h1_ref, held_ref, m0_ref, m1_ref):
    blocks, slots = fmask_ref.shape
    for i in range(blocks):
        rows = pl.ds(i * size, size)
        for o in range(slots):
            cols = pl.ds(o * size, size)
            tile = fock_ref[rows, cols]
            held_ref[rows, cols] = jnp.where(fmask_ref[i, o] != 0, tile, jnp.zeros_like(tile))
        fock = held_ref[rows, pl.ds((blocks - i) * size, blocks * size)]
        m0_ref[rows, :] = dot(fock, h0_ref[...])
        m1_ref[rows, :] = dot(fock, h1_ref[...])


def pick_kernel(edge, own_ref, crossed_ref, up_ref, down_ref):
    y, z = lax.axis_index("y"), lax.axis_index("z")
    top, bottom = (y == edge[0] - 1) & (z == edge[1] - 1), (y == 0) & (z == 0)
    for ref, cross in ((up_ref, top), (down_ref, bottom)):

        @pl.when(cross)
        def _():
            ref[...] = crossed_ref[...]

        @pl.when(jnp.logical_not(cross))
        def _():
            ref[...] = own_ref[...]


def near_kernel(size, h, rmask_ref, held_ref, mid_ref, low_ref, high_ref, *rest):
    own_refs, near_ref, rest = rest[:2], rest[2], rest[3:]
    start = 0
    if h == 1:
        first_ref, earlier_ref, rest = rest[0], rest[1], rest[2:]
        start = first_ref.shape[1]
    out_ref, outt_ref, terms_ref = rest
    if h == 1:
        out_ref[:, :start] = first_ref[...]
        terms_ref[:, :start, :] = earlier_ref[...]
    blocks = rmask_ref.shape[1]
    slots = held_ref.shape[1] // size
    panels = mid_ref.shape[1] // size
    for i in range(blocks):
        rows = pl.ds(i * size, size)
        total = mid_ref[rows, :]
        total += dot(held_ref[rows, : (blocks - i) * size], low_ref[i * size :, :])
        total += dot(held_ref[rows, (2 * blocks - i) * size :], high_ref[: (slots - 2 * blocks + i) * size, :])
        for j in range(panels):
            cols = slice(j * size, (j + 1) * size)
            tile = total[:, cols]
            keep = rmask_ref[h * panels + j, i] != 0
            tile = jnp.where(keep, tile, jnp.zeros_like(tile)).astype(BF16)
            out_ref[rows, pl.ds(start + j * size, size)] = tile
            outt_ref[cols, rows] = tile.T
    core, deep = lax.axis_index("core"), pl.ds(start, outt_ref.shape[0])
    for k in range(2):
        terms_ref[core * 2 + k, deep, :] = dot(outt_ref[...], own_refs[k][...]).astype(BF16)
        terms_ref[(1 - core) * 2 + k, deep, :] = dot(outt_ref[...], near_ref[k]).astype(BF16)


def far_kernel(t0_ref, t1_ref, far_ref, terms_ref):
    half = t0_ref.shape[0]
    for c in range(2):
        for k, t in enumerate((t0_ref, t1_ref)):
            terms_ref[c, pl.ds(k * half, half), :] = dot(t[...], far_ref[c]).astype(BF16)


def gather_kernel(t0_ref, t1_ref, both_ref, near_ref, far_ref, out_ref):
    half = t0_ref.shape[0]
    core = lax.axis_index("core")
    late = pl.ds(half, half)
    for c in range(2):
        out_ref[core * 2 + c, :, late] = far_ref[c]
        for k, t in enumerate((t0_ref, t1_ref)):
            out_ref[(1 - core) * 2 + c, pl.ds(k * half, half), late] = dot(t[...], both_ref[c]).astype(BF16)
    out_ref[:, :, :half] = near_ref[...]


def first_sum_kernel(in_ref, out_ref):
    count, deep, _ = out_ref.shape
    inner = count // 2
    xh = lax.axis_index("xh")
    total = in_ref[0].astype(F32)
    for s in range(1, in_ref.shape[0]):
        total += in_ref[s].astype(F32)
    half = total.shape[1] // 2
    for f in range(2):
        turned = total[:, f * half : (f + 1) * half].T.astype(BF16)
        for z in range(inner):
            out_ref[(xh ^ f) * inner + z] = turned[z * deep : (z + 1) * deep]


def last_sum_kernel(factor, in_ref, out_ref):
    total = in_ref[0].astype(F32)
    for s in range(1, in_ref.shape[0]):
        total += in_ref[s].astype(F32)
    out_ref[...] = total * factor


def after(x, *others):
    anywhere = pl.BlockSpec(memory_space=pl.ANY)
    return pl.pallas_call(
        lambda *refs: None,
        out_shape=jax.ShapeDtypeStruct(x.shape, x.dtype),
        in_specs=[anywhere] * (1 + len(others)),
        out_specs=anywhere,
        input_output_aliases={0: 0},
        compiler_params=pltpu.CompilerParams(vmem_limit_bytes=MIB),
    )(x, *others)


def ring(count, step):
    return [(i, (i + step) % count) for i in range(count)]


def on_device(fock_band, fock_slot_mask, orbital_slab, orbital_mask, result_mask):
    blocks, slots = fock_slot_mask.shape
    rows, columns = orbital_slab.shape
    size = rows // blocks
    half = columns // 2
    like = jax.ShapeDtypeStruct
    groups, wide, deep = lax.axis_size(ROWS), lax.axis_size("y"), lax.axis_size("z")
    plane = wide * deep
    piece = like((rows, half), BF16)
    h0, h1, panels = call(
        functools.partial(mask_kernel, size),
        (piece, piece, like((2, rows, half), BF16)),
        [SMEM, HBM],
        [
            pltpu.VMEM((rows, columns), BF16),
            pltpu.VMEM((2, rows, half), BF16),
            pltpu.SemaphoreType.DMA((blocks,)),
            pltpu.SemaphoreType.DMA((blocks, 4)),
        ],
        limit=60 * MIB,
        place=HBM,
    )(orbital_mask.T, orbital_slab)
    swap = ring(2, 1)
    low0 = lax.ppermute(h0, ROWS, ring(groups, 1))
    high0 = lax.ppermute(h0, ROWS, ring(groups, groups - 1))
    ends = [(i, (i + plane) % groups) for i in range(groups) if i % plane in (0, plane - 1)]
    crossed = lax.ppermute(h1, ROWS, ends)
    far = lax.ppermute(panels, "xh", swap)
    near_panels = lax.ppermute(panels, "core", swap)
    held, mid0, mid1 = call(
        functools.partial(middle_kernel, size),
        (like((rows, slots * size), BF16), *[like((rows, half), F32)] * 2),
        [SMEM, VMEM, VMEM, VMEM],
        flops=2 * rows * rows * columns,
        moved=4 * rows * slots * size,
    )(fock_slot_mask, fock_band, h0, h1)
    up1, down1 = call(
        functools.partial(pick_kernel, (wide, deep)), (piece, piece), [VMEM, VMEM], moved=8 * rows * half
    )(h1, after(crossed, near_panels))
    within = [(i, i + 1 if (i + 1) % plane else i + 1 - plane) for i in range(groups)]
    low1 = lax.ppermute(up1, ROWS, within)
    high1 = lax.ppermute(down1, ROWS, [(b, a) for a, b in within])

    def near(h, mid, low, high, *first):
        width = half if h == 0 else columns
        return call(
            functools.partial(near_kernel, size, h),
            (like((rows, width), BF16), like((half, rows), BF16), like((wide, width, half), BF16)),
            [SMEM] + [VMEM] * (7 + len(first)),
            flops=2 * rows * half * (2 * columns + (slots - blocks) * size),
            moved=8 * rows * columns,
        )(result_mask.T, held, mid, low, high, h0, h1, near_panels, *first)

    product0, flipped0, terms0 = near(0, mid0, low0, high0)
    product, flipped1, terms1 = near(1, mid1, low1, high1, product0, terms0)
    far = after(far, terms1)
    both = lax.ppermute(far, "core", swap)
    far_terms = call(
        far_kernel,
        like((2, columns, half), BF16),
        [VMEM] * 3,
        flops=4 * rows * half * columns,
        moved=8 * rows * half,
    )(flipped0, flipped1, far)
    terms = call(
        gather_kernel,
        like((wide, columns, columns), BF16),
        [VMEM] * 5,
        flops=4 * rows * half * columns,
        moved=8 * rows * columns,
    )(flipped0, flipped1, both, terms1, far_terms)
    terms = lax.all_to_all(terms, "y", 0, 0, tiled=True)
    part = call(first_sum_kernel, like((2 * deep, half // deep, columns), BF16), [VMEM])(terms)
    part = lax.all_to_all(part, ("xl", "z"), 0, 0, tiled=True)
    factor = 1.0 / math.sqrt(rows * groups)
    projected = call(
        functools.partial(last_sum_kernel, factor), like((half // deep, columns), F32), [VMEM]
    )(part)
    return (product, projected)


def solution(mesh):
    split = Mesh(mesh.devices.reshape(2, 2, 2, 4, 8), BLK + ROWS)
    placed = (P(ROWS, None), P(ROWS, None), P(ROWS, BLK), P(ROWS, BLK), P(ROWS, BLK))
    return jax.shard_map(
        on_device,
        mesh=split,
        in_specs=placed,
        out_specs=(P(ROWS, BLK), P(ROWS, BLK)),
        check_vma=False,
    )
```

```python
import functools
import math

import jax
import jax.numpy as jnp
from jax import lax
from jax.experimental import pallas as pl
from jax.experimental.pallas import tpu as pltpu
from jax.sharding import Mesh, PartitionSpec as P

F32, BF16 = jnp.float32, jnp.bfloat16
ROWS = ("xl", "y", "z")
BLK = ("xh", "core")
VMEM = pl.BlockSpec(memory_space=pltpu.VMEM)
SMEM = pl.BlockSpec(memory_space=pltpu.SMEM)
HBM = pl.BlockSpec(memory_space=pltpu.HBM)
MIB = 1 << 20


def call(body, outs, ins, scratch=(), limit=8 * MIB, flops=0, moved=0, place=VMEM):
    return pl.pallas_call(
        body,
        out_shape=outs,
        in_specs=ins,
        out_specs=jax.tree.map(lambda _: place, outs),
        scratch_shapes=list(scratch),
        compiler_params=pltpu.CompilerParams(vmem_limit_bytes=limit),
        cost_estimate=pl.CostEstimate(flops=flops, bytes_accessed=moved, transcendentals=0),
    )


def dot(a, b):
    return jnp.dot(a, b, preferred_element_type=F32)


def mask_kernel(size, mask_hbm, slab_hbm, h0_hbm, h1_hbm, both_hbm, mask_ref, loaded, kept, mask_sem, in_sems, out_sems):
    panels, blocks = mask_ref.shape
    mask_load = pltpu.make_async_copy(mask_hbm, mask_ref, mask_sem)
    mask_load.start()
    half = panels // 2
    at = [pl.ds(i * size, size) for i in range(blocks)]
    loads = [pltpu.make_async_copy(slab_hbm.at[at[i]], loaded.at[at[i]], in_sems.at[i]) for i in range(blocks)]
    for load in loads:
        load.start()
    mask_load.wait()
    stores = []
    for i, load in enumerate(loads):
        load.wait()
        for j in range(panels):
            tile = loaded[at[i], pl.ds(j * size, size)]
            tile = jnp.where(mask_ref[j, i] != 0, tile, jnp.zeros_like(tile))
            kept[j // half, at[i], pl.ds((j % half) * size, size)] = tile
        for h, ref in enumerate((h0_hbm, h1_hbm)):
            stores.append(pltpu.make_async_copy(kept.at[h, at[i]], ref.at[at[i]], out_sems.at[i, 2 * h]))
            stores.append(pltpu.make_async_copy(kept.at[h, at[i]], both_hbm.at[h, at[i]], out_sems.at[i, 2 * h + 1]))
        for store in stores[-4:]:
            store.start()
    for store in stores:
        store.wait()


def middle_kernel(size, fmask_ref, fock_ref, h0_ref, h1_ref, held_ref, m0_ref, m1_ref):
    blocks, slots = fmask_ref.shape
    for i in range(blocks):
        rows = pl.ds(i * size, size)
        for o in range(slots):
            cols = pl.ds(o * size, size)
            tile = fock_ref[rows, cols]
            held_ref[rows, cols] = jnp.where(fmask_ref[i, o] != 0, tile, jnp.zeros_like(tile))
        fock = held_ref[rows, pl.ds((blocks - i) * size, blocks * size)]
        m0_ref[rows, :] = dot(fock, h0_ref[...])
        m1_ref[rows, :] = dot(fock, h1_ref[...])


def pick_kernel(edge, own_ref, crossed_ref, up_ref, down_ref):
    y, z = lax.axis_index("y"), lax.axis_index("z")
    top, bottom = (y == edge[0] - 1) & (z == edge[1] - 1), (y == 0) & (z == 0)
    for ref, cross in ((up_ref, top), (down_ref, bottom)):

        @pl.when(cross)
        def _():
            ref[...] = crossed_ref[...]

        @pl.when(jnp.logical_not(cross))
        def _():
            ref[...] = own_ref[...]


def near_kernel(size, h, rmask_ref, held_ref, mid_ref, low_ref, high_ref, *rest):
    own_refs, near_ref, rest = rest[:2], rest[2], rest[3:]
    start = 0
    if h == 1:
        first_ref, rest = rest[0], rest[1:]
        start = first_ref.shape[1]
    out_ref, outt_ref, terms_ref = rest
    if h == 1:
        out_ref[:, :start] = first_ref[...]
    blocks = rmask_ref.shape[1]
    slots = held_ref.shape[1] // size
    panels = mid_ref.shape[1] // size
    for i in range(blocks):
        rows = pl.ds(i * size, size)
        total = mid_ref[rows, :]
        total += dot(held_ref[rows, : (blocks - i) * size], low_ref[i * size :, :])
        total += dot(held_ref[rows, (2 * blocks - i) * size :], high_ref[: (slots - 2 * blocks + i) * size, :])
        for j in range(panels):
            cols = slice(j * size, (j + 1) * size)
            tile = total[:, cols]
            keep = rmask_ref[h * panels + j, i] != 0
            tile = jnp.where(keep, tile, jnp.zeros_like(tile)).astype(BF16)
            out_ref[rows, pl.ds(start + j * size, size)] = tile
            outt_ref[cols, rows] = tile.T
    core = lax.axis_index("core")
    for k in range(2):
        terms_ref[core * 2 + k] = dot(outt_ref[...], own_refs[k][...]).astype(BF16)
        terms_ref[(1 - core) * 2 + k] = dot(outt_ref[...], near_ref[k]).astype(BF16)


def far_kernel(t0_ref, t1_ref, far_ref, terms_ref):
    half = t0_ref.shape[0]
    for c in range(2):
        for k, t in enumerate((t0_ref, t1_ref)):
            terms_ref[c, pl.ds(k * half, half), :] = dot(t[...], far_ref[c]).astype(BF16)


def gather_kernel(t0_ref, t1_ref, both_ref, near0_ref, near1_ref, far_ref, out_ref):
    half = t0_ref.shape[0]
    core, xh = lax.axis_index("core"), lax.axis_index("xh")
    other = (1 - xh) * 4
    for c in range(2):
        out_ref[other + core * 2 + c] = far_ref[c]
        for k, t in enumerate((t0_ref, t1_ref)):
            out_ref[other + (1 - core) * 2 + c, pl.ds(k * half, half), :] = dot(t[...], both_ref[c]).astype(BF16)
    for s in range(4):
        for k, ref in enumerate((near0_ref, near1_ref)):
            out_ref[xh * 4 + s, pl.ds(k * half, half), :] = ref[s]


def first_sum_kernel(in_ref, out_ref):
    total = in_ref[0].astype(F32)
    for s in range(1, in_ref.shape[0]):
        total += in_ref[s].astype(F32)
    out_ref[...] = total.T.astype(BF16)


def last_sum_kernel(factor, in_ref, out_ref):
    total = in_ref[0].astype(F32)
    for s in range(1, in_ref.shape[0]):
        total += in_ref[s].astype(F32)
    out_ref[...] = total * factor


def after(x, *others):
    anywhere = pl.BlockSpec(memory_space=pl.ANY)
    return pl.pallas_call(
        lambda *refs: None,
        out_shape=jax.ShapeDtypeStruct(x.shape, x.dtype),
        in_specs=[anywhere] * (1 + len(others)),
        out_specs=anywhere,
        input_output_aliases={0: 0},
        compiler_params=pltpu.CompilerParams(vmem_limit_bytes=MIB),
    )(x, *others)


def ring(count, step):
    return [(i, (i + step) % count) for i in range(count)]


def on_device(fock_band, fock_slot_mask, orbital_slab, orbital_mask, result_mask):
    blocks, slots = fock_slot_mask.shape
    rows, columns = orbital_slab.shape
    size = rows // blocks
    half = columns // 2
    like = jax.ShapeDtypeStruct
    groups, wide, deep = lax.axis_size(ROWS), lax.axis_size("y"), lax.axis_size("z")
    plane = wide * deep
    piece = like((rows, half), BF16)
    h0, h1, panels = call(
        functools.partial(mask_kernel, size),
        (piece, piece, like((2, rows, half), BF16)),
        [HBM, HBM],
        [
            pltpu.SMEM(orbital_mask.shape[::-1], jnp.int32),
            pltpu.VMEM((rows, columns), BF16),
            pltpu.VMEM((2, rows, half), BF16),
            pltpu.SemaphoreType.DMA,
            pltpu.SemaphoreType.DMA((blocks,)),
            pltpu.SemaphoreType.DMA((blocks, 4)),
        ],
        limit=60 * MIB,
        place=HBM,
    )(orbital_mask.T, orbital_slab)
    swap = ring(2, 1)
    low0 = lax.ppermute(h0, ROWS, ring(groups, 1))
    high0 = lax.ppermute(h0, ROWS, ring(groups, groups - 1))
    ends = [(i, (i + plane) % groups) for i in range(groups) if i % plane in (0, plane - 1)]
    crossed = lax.ppermute(h1, ROWS, ends)
    far = lax.ppermute(panels, "xh", swap)
    near_panels = lax.ppermute(panels, "core", swap)
    held, mid0, mid1 = call(
        functools.partial(middle_kernel, size),
        (like((rows, slots * size), BF16), *[like((rows, half), F32)] * 2),
        [SMEM, VMEM, VMEM, VMEM],
        flops=2 * rows * rows * columns,
        moved=4 * rows * slots * size,
    )(fock_slot_mask, fock_band, h0, h1)
    up1, down1 = call(
        functools.partial(pick_kernel, (wide, deep)), (piece, piece), [VMEM, VMEM], moved=8 * rows * half
    )(h1, after(crossed, near_panels))
    within = [(i, i + 1 if (i + 1) % plane else i + 1 - plane) for i in range(groups)]
    low1 = lax.ppermute(up1, ROWS, within)
    high1 = lax.ppermute(down1, ROWS, [(b, a) for a, b in within])

    def near(h, mid, low, high, *first):
        width = half if h == 0 else columns
        return call(
            functools.partial(near_kernel, size, h),
            (like((rows, width), BF16), like((half, rows), BF16), like((4, half, half), BF16)),
            [SMEM] + [VMEM] * (7 + len(first)),
            flops=2 * rows * half * (2 * columns + (slots - blocks) * size),
            moved=8 * rows * columns,
        )(result_mask.T, held, mid, low, high, h0, h1, near_panels, *first)

    product0, flipped0, terms0 = near(0, mid0, low0, high0)
    product, flipped1, terms1 = near(1, mid1, low1, high1, product0)
    far = after(far, terms1)
    both = lax.ppermute(far, "core", swap)
    far_terms = call(
        far_kernel,
        like((2, columns, half), BF16),
        [VMEM] * 3,
        flops=4 * rows * half * columns,
        moved=8 * rows * half,
    )(flipped0, flipped1, far)
    terms = call(
        gather_kernel,
        like((groups // deep, columns, half), BF16),
        [VMEM] * 6,
        flops=4 * rows * half * columns,
        moved=8 * rows * columns,
    )(flipped0, flipped1, both, terms0, terms1, far_terms)
    terms = lax.all_to_all(terms, ("xl", "y"), 0, 0, tiled=True)
    part = call(first_sum_kernel, like((half, columns), BF16), [VMEM])(terms)
    part = part.reshape(deep, half // deep, columns)
    part = lax.all_to_all(part, "z", 0, 0, tiled=True)
    factor = 1.0 / math.sqrt(rows * groups)
    projected = call(
        functools.partial(last_sum_kernel, factor), like((half // deep, columns), F32), [VMEM]
    )(part)
    return (product, projected)


def solution(mesh):
    split = Mesh(mesh.devices.reshape(2, 2, 2, 4, 8), BLK + ROWS)
    placed = (P(ROWS, None), P(ROWS, None), P(ROWS, BLK), P(ROWS, BLK), P(ROWS, BLK))
    return jax.shard_map(
        on_device,
        mesh=split,
        in_specs=placed,
        out_specs=(P(ROWS, BLK), P(ROWS, BLK)),
        check_vma=False,
    )
```

```python
import functools
import math

import jax
import jax.numpy as jnp
from jax import lax
from jax.experimental import pallas as pl
from jax.experimental.pallas import tpu as pltpu
from jax.sharding import Mesh, PartitionSpec as P

F32, BF16 = jnp.float32, jnp.bfloat16
ROWS = ("xl", "y", "z")
BLK = ("xh", "core")
VMEM = pl.BlockSpec(memory_space=pltpu.VMEM)
SMEM = pl.BlockSpec(memory_space=pltpu.SMEM)
HBM = pl.BlockSpec(memory_space=pltpu.HBM)
MIB = 1 << 20


def call(body, outs, ins, scratch=(), limit=8 * MIB, flops=0, moved=0, place=VMEM):
    return pl.pallas_call(
        body,
        out_shape=outs,
        in_specs=ins,
        out_specs=jax.tree.map(lambda _: place, outs),
        scratch_shapes=list(scratch),
        compiler_params=pltpu.CompilerParams(vmem_limit_bytes=limit),
        cost_estimate=pl.CostEstimate(flops=flops, bytes_accessed=moved, transcendentals=0),
    )


def dot(a, b):
    return jnp.dot(a, b, preferred_element_type=F32)


def mask_kernel(size, mask_hbm, slab_hbm, h0_hbm, h1_hbm, both_hbm, mask_ref, loaded, kept, mask_sem, in_sems, out_sems):
    panels, blocks = mask_ref.shape
    mask_load = pltpu.make_async_copy(mask_hbm, mask_ref, mask_sem)
    mask_load.start()
    half = panels // 2
    at = [pl.ds(i * size, size) for i in range(blocks)]
    loads = [pltpu.make_async_copy(slab_hbm.at[at[i]], loaded.at[at[i]], in_sems.at[i]) for i in range(blocks)]
    for load in loads:
        load.start()
    mask_load.wait()
    stores = []
    for i, load in enumerate(loads):
        load.wait()
        for j in range(panels):
            tile = loaded[at[i], pl.ds(j * size, size)]
            tile = jnp.where(mask_ref[j, i] != 0, tile, jnp.zeros_like(tile))
            kept[j // half, at[i], pl.ds((j % half) * size, size)] = tile
        for h, ref in enumerate((h0_hbm, h1_hbm)):
            stores.append(pltpu.make_async_copy(kept.at[h, at[i]], ref.at[at[i]], out_sems.at[i, 2 * h]))
            stores.append(pltpu.make_async_copy(kept.at[h, at[i]], both_hbm.at[h, at[i]], out_sems.at[i, 2 * h + 1]))
        for store in stores[-4:]:
            store.start()
    for store in stores:
        store.wait()


def middle_kernel(size, fmask_ref, fock_ref, h0_ref, h1_ref, held_ref, m0_ref, m1_ref):
    blocks, slots = fmask_ref.shape
    for i in range(blocks):
        rows = pl.ds(i * size, size)
        for o in range(slots):
            cols = pl.ds(o * size, size)
            tile = fock_ref[rows, cols]
            held_ref[rows, cols] = jnp.where(fmask_ref[i, o] != 0, tile, jnp.zeros_like(tile))
        fock = held_ref[rows, pl.ds((blocks - i) * size, blocks * size)]
        m0_ref[rows, :] = dot(fock, h0_ref[...])
        m1_ref[rows, :] = dot(fock, h1_ref[...])


def pick_kernel(edge, own_ref, crossed_ref, up_ref, down_ref):
    y, z = lax.axis_index("y"), lax.axis_index("z")
    top, bottom = (y == edge[0] - 1) & (z == edge[1] - 1), (y == 0) & (z == 0)
    for ref, cross in ((up_ref, top), (down_ref, bottom)):

        @pl.when(cross)
        def _():
            ref[...] = crossed_ref[...]

        @pl.when(jnp.logical_not(cross))
        def _():
            ref[...] = own_ref[...]


def near_kernel(size, h, rmask_ref, held_ref, mid_ref, low_ref, high_ref, *rest):
    own_refs, near_ref, rest = rest[:2], rest[2], rest[3:]
    start = 0
    if h == 1:
        first_ref, rest = rest[0], rest[1:]
        start = first_ref.shape[1]
    out_ref, outt_ref, terms_ref = rest
    if h == 1:
        out_ref[:, :start] = first_ref[...]
    blocks = rmask_ref.shape[1]
    slots = held_ref.shape[1] // size
    panels = mid_ref.shape[1] // size
    for i in range(blocks):
        rows = pl.ds(i * size, size)
        total = mid_ref[rows, :]
        total += dot(held_ref[rows, : (blocks - i) * size], low_ref[i * size :, :])
        total += dot(held_ref[rows, (2 * blocks - i) * size :], high_ref[: (slots - 2 * blocks + i) * size, :])
        for j in range(panels):
            cols = slice(j * size, (j + 1) * size)
            tile = total[:, cols]
            keep = rmask_ref[h * panels + j, i] != 0
            tile = jnp.where(keep, tile, jnp.zeros_like(tile)).astype(BF16)
            out_ref[rows, pl.ds(start + j * size, size)] = tile
            outt_ref[cols, rows] = tile.T
    core = lax.axis_index("core")
    for k in range(2):
        terms_ref[core * 2 + k] = dot(outt_ref[...], own_refs[k][...]).astype(BF16)
        terms_ref[(1 - core) * 2 + k] = dot(outt_ref[...], near_ref[k]).astype(BF16)


def far_kernel(t0_ref, t1_ref, far_ref, terms_ref):
    half = t0_ref.shape[0]
    for c in range(2):
        for k, t in enumerate((t0_ref, t1_ref)):
            terms_ref[c, pl.ds(k * half, half), :] = dot(t[...], far_ref[c]).astype(BF16)


def gather_kernel(t0_ref, t1_ref, both_ref, near0_ref, near1_ref, far_ref, out_ref):
    half = t0_ref.shape[0]
    core, xh = lax.axis_index("core"), lax.axis_index("xh")
    other = (1 - xh) * 4
    for c in range(2):
        out_ref[other + core * 2 + c] = far_ref[c]
        for k, t in enumerate((t0_ref, t1_ref)):
            out_ref[other + (1 - core) * 2 + c, pl.ds(k * half, half), :] = dot(t[...], both_ref[c]).astype(BF16)
    for s in range(4):
        for k, ref in enumerate((near0_ref, near1_ref)):
            out_ref[xh * 4 + s, pl.ds(k * half, half), :] = ref[s]


def first_sum_kernel(in_ref, out_ref):
    total = in_ref[0].astype(F32)
    for s in range(1, in_ref.shape[0]):
        total += in_ref[s].astype(F32)
    out_ref[...] = total.T.astype(BF16)


def last_sum_kernel(factor, in_ref, out_ref):
    total = in_ref[0].astype(F32)
    for s in range(1, in_ref.shape[0]):
        total += in_ref[s].astype(F32)
    out_ref[...] = total * factor


def after(x, *others):
    anywhere = pl.BlockSpec(memory_space=pl.ANY)
    return pl.pallas_call(
        lambda *refs: None,
        out_shape=jax.ShapeDtypeStruct(x.shape, x.dtype),
        in_specs=[anywhere] * (1 + len(others)),
        out_specs=anywhere,
        input_output_aliases={0: 0},
        compiler_params=pltpu.CompilerParams(vmem_limit_bytes=MIB),
    )(x, *others)


def ring(count, step):
    return [(i, (i + step) % count) for i in range(count)]


def on_device(fock_band, fock_slot_mask, orbital_slab, orbital_mask, result_mask):
    blocks, slots = fock_slot_mask.shape
    rows, columns = orbital_slab.shape
    size = rows // blocks
    half = columns // 2
    like = jax.ShapeDtypeStruct
    groups, wide, deep = lax.axis_size(ROWS), lax.axis_size("y"), lax.axis_size("z")
    plane = wide * deep
    piece = like((rows, half), BF16)
    h0, h1, panels = call(
        functools.partial(mask_kernel, size),
        (piece, piece, like((2, rows, half), BF16)),
        [HBM, HBM],
        [
            pltpu.SMEM(orbital_mask.shape[::-1], jnp.int32),
            pltpu.VMEM((rows, columns), BF16),
            pltpu.VMEM((2, rows, half), BF16),
            pltpu.SemaphoreType.DMA,
            pltpu.SemaphoreType.DMA((blocks,)),
            pltpu.SemaphoreType.DMA((blocks, 4)),
        ],
        limit=60 * MIB,
        place=HBM,
    )(orbital_mask.T, orbital_slab)
    swap = ring(2, 1)
    low0 = lax.ppermute(h0, ROWS, ring(groups, 1))
    high0 = lax.ppermute(h0, ROWS, ring(groups, groups - 1))
    far_ends = (0, plane - 1)
    ends = [(i, (i + plane) % groups if i % plane in far_ends else i) for i in range(groups)]
    crossed = lax.ppermute(h1, ROWS, ends)
    far = lax.ppermute(panels, "xh", swap)
    near_panels = lax.ppermute(panels, "core", swap)
    held, mid0, mid1 = call(
        functools.partial(middle_kernel, size),
        (like((rows, slots * size), BF16), *[like((rows, half), F32)] * 2),
        [SMEM, VMEM, VMEM, VMEM],
        flops=2 * rows * rows * columns,
        moved=4 * rows * slots * size,
    )(fock_slot_mask, fock_band, h0, h1)
    up1, down1 = call(
        functools.partial(pick_kernel, (wide, deep)), (piece, piece), [VMEM, VMEM], moved=8 * rows * half
    )(h1, after(crossed, near_panels))
    within = [(i, i + 1 if (i + 1) % plane else i + 1 - plane) for i in range(groups)]
    low1 = lax.ppermute(up1, ROWS, within)
    high1 = lax.ppermute(down1, ROWS, [(b, a) for a, b in within])

    def near(h, mid, low, high, *first):
        width = half if h == 0 else columns
        return call(
            functools.partial(near_kernel, size, h),
            (like((rows, width), BF16), like((half, rows), BF16), like((4, half, half), BF16)),
            [SMEM] + [VMEM] * (7 + len(first)),
            flops=2 * rows * half * (2 * columns + (slots - blocks) * size),
            moved=8 * rows * columns,
        )(result_mask.T, held, mid, low, high, h0, h1, near_panels, *first)

    product0, flipped0, terms0 = near(0, mid0, low0, high0)
    product, flipped1, terms1 = near(1, mid1, low1, high1, product0)
    far = after(far, terms1)
    both = lax.ppermute(far, "core", swap)
    far_terms = call(
        far_kernel,
        like((2, columns, half), BF16),
        [VMEM] * 3,
        flops=4 * rows * half * columns,
        moved=8 * rows * half,
    )(flipped0, flipped1, far)
    terms = call(
        gather_kernel,
        like((groups // deep, columns, half), BF16),
        [VMEM] * 6,
        flops=4 * rows * half * columns,
        moved=8 * rows * columns,
    )(flipped0, flipped1, both, terms0, terms1, far_terms)
    terms = lax.all_to_all(terms, ("xl", "y"), 0, 0, tiled=True)
    part = call(first_sum_kernel, like((half, columns), BF16), [VMEM])(terms)
    part = part.reshape(deep, half // deep, columns)
    part = lax.all_to_all(part, "z", 0, 0, tiled=True)
    factor = 1.0 / math.sqrt(rows * groups)
    projected = call(
        functools.partial(last_sum_kernel, factor), like((half // deep, columns), F32), [VMEM]
    )(part)
    return (product, projected)


def solution(mesh):
    split = Mesh(mesh.devices.reshape(2, 2, 2, 4, 8), BLK + ROWS)
    placed = (P(ROWS, None), P(ROWS, None), P(ROWS, BLK), P(ROWS, BLK), P(ROWS, BLK))
    return jax.shard_map(
        on_device,
        mesh=split,
        in_specs=placed,
        out_specs=(P(ROWS, BLK), P(ROWS, BLK)),
        check_vma=False,
    )
```

```python
import functools
import math

import jax
import jax.numpy as jnp
from jax import lax
from jax.experimental import pallas as pl
from jax.experimental.pallas import tpu as pltpu
from jax.sharding import Mesh, PartitionSpec as P

F32, BF16 = jnp.float32, jnp.bfloat16
ROWS = ("xl", "y", "z")
BLK = ("xh", "core")
VMEM = pl.BlockSpec(memory_space=pltpu.VMEM)
SMEM = pl.BlockSpec(memory_space=pltpu.SMEM)
HBM = pl.BlockSpec(memory_space=pltpu.HBM)
MIB = 1 << 20


def call(body, outs, ins, scratch=(), limit=8 * MIB, flops=0, moved=0, place=VMEM):
    return pl.pallas_call(
        body,
        out_shape=outs,
        in_specs=ins,
        out_specs=jax.tree.map(lambda _: place, outs),
        scratch_shapes=list(scratch),
        compiler_params=pltpu.CompilerParams(vmem_limit_bytes=limit),
        cost_estimate=pl.CostEstimate(flops=flops, bytes_accessed=moved, transcendentals=0),
    )


def dot(a, b):
    return jnp.dot(a, b, preferred_element_type=F32)


def mask_kernel(size, mask_hbm, slab_hbm, h0_hbm, h1_hbm, both_hbm, mask_ref, loaded, kept, mask_sem, in_sems, out_sems):
    panels, blocks = mask_ref.shape
    mask_load = pltpu.make_async_copy(mask_hbm, mask_ref, mask_sem)
    mask_load.start()
    half = panels // 2
    pieces = in_sems.shape[0]
    span = blocks // pieces
    at = [pl.ds(i * span * size, span * size) for i in range(pieces)]
    loads = [pltpu.make_async_copy(slab_hbm.at[at[i]], loaded.at[at[i]], in_sems.at[i]) for i in range(pieces)]
    for load in loads:
        load.start()
    mask_load.wait()
    stores = []
    for i, load in enumerate(loads):
        load.wait()
        for j in range(panels):
            for b in range(i * span, (i + 1) * span):
                rows = pl.ds(b * size, size)
                tile = loaded[rows, pl.ds(j * size, size)]
                tile = jnp.where(mask_ref[j, b] != 0, tile, jnp.zeros_like(tile))
                kept[j // half, rows, pl.ds((j % half) * size, size)] = tile
        for h, ref in enumerate((h0_hbm, h1_hbm)):
            stores.append(pltpu.make_async_copy(kept.at[h, at[i]], ref.at[at[i]], out_sems.at[i, 2 * h]))
            stores.append(pltpu.make_async_copy(kept.at[h, at[i]], both_hbm.at[h, at[i]], out_sems.at[i, 2 * h + 1]))
        for store in stores[-4:]:
            store.start()
    for store in stores:
        store.wait()


def middle_kernel(size, fmask_ref, fock_ref, h0_ref, h1_ref, held_ref, m0_ref, m1_ref):
    blocks, slots = fmask_ref.shape
    for i in range(blocks):
        rows = pl.ds(i * size, size)
        for o in range(slots):
            cols = pl.ds(o * size, size)
            tile = fock_ref[rows, cols]
            held_ref[rows, cols] = jnp.where(fmask_ref[i, o] != 0, tile, jnp.zeros_like(tile))
        fock = held_ref[rows, pl.ds((blocks - i) * size, blocks * size)]
        m0_ref[rows, :] = dot(fock, h0_ref[...])
        m1_ref[rows, :] = dot(fock, h1_ref[...])


def pick_kernel(edge, own_ref, crossed_ref, up_ref, down_ref):
    y, z = lax.axis_index("y"), lax.axis_index("z")
    top, bottom = (y == edge[0] - 1) & (z == edge[1] - 1), (y == 0) & (z == 0)
    for ref, cross in ((up_ref, top), (down_ref, bottom)):

        @pl.when(cross)
        def _():
            ref[...] = crossed_ref[...]

        @pl.when(jnp.logical_not(cross))
        def _():
            ref[...] = own_ref[...]


def near_kernel(size, h, rmask_ref, held_ref, mid_ref, low_ref, high_ref, *rest):
    own_refs, near_ref, rest = rest[:2], rest[2], rest[3:]
    start = 0
    if h == 1:
        first_ref, rest = rest[0], rest[1:]
        start = first_ref.shape[1]
    out_ref, outt_ref, terms_ref = rest
    if h == 1:
        out_ref[:, :start] = first_ref[...]
    blocks = rmask_ref.shape[1]
    slots = held_ref.shape[1] // size
    panels = mid_ref.shape[1] // size
    for i in range(blocks):
        rows = pl.ds(i * size, size)
        total = mid_ref[rows, :]
        total += dot(held_ref[rows, : (blocks - i) * size], low_ref[i * size :, :])
        total += dot(held_ref[rows, (2 * blocks - i) * size :], high_ref[: (slots - 2 * blocks + i) * size, :])
        for j in range(panels):
            cols = slice(j * size, (j + 1) * size)
            tile = total[:, cols]
            keep = rmask_ref[h * panels + j, i] != 0
            tile = jnp.where(keep, tile, jnp.zeros_like(tile)).astype(BF16)
            out_ref[rows, pl.ds(start + j * size, size)] = tile
            outt_ref[cols, rows] = tile.T
    core = lax.axis_index("core")
    for k in range(2):
        terms_ref[core * 2 + k] = dot(outt_ref[...], own_refs[k][...]).astype(BF16)
        terms_ref[(1 - core) * 2 + k] = dot(outt_ref[...], near_ref[k]).astype(BF16)


def far_kernel(t0_ref, t1_ref, far_ref, terms_ref):
    half = t0_ref.shape[0]
    for c in range(2):
        for k, t in enumerate((t0_ref, t1_ref)):
            terms_ref[c, pl.ds(k * half, half), :] = dot(t[...], far_ref[c]).astype(BF16)


def gather_kernel(t0_ref, t1_ref, both_ref, near0_ref, near1_ref, far_ref, out_ref):
    half = t0_ref.shape[0]
    core, xh = lax.axis_index("core"), lax.axis_index("xh")
    other = (1 - xh) * 4
    for c in range(2):
        out_ref[other + core * 2 + c] = far_ref[c]
        for k, t in enumerate((t0_ref, t1_ref)):
            out_ref[other + (1 - core) * 2 + c, pl.ds(k * half, half), :] = dot(t[...], both_ref[c]).astype(BF16)
    for s in range(4):
        for k, ref in enumerate((near0_ref, near1_ref)):
            out_ref[xh * 4 + s, pl.ds(k * half, half), :] = ref[s]


def first_sum_kernel(in_ref, out_ref):
    total = in_ref[0].astype(F32)
    for s in range(1, in_ref.shape[0]):
        total += in_ref[s].astype(F32)
    out_ref[...] = total.T.astype(BF16)


def last_sum_kernel(factor, in_ref, out_ref):
    total = in_ref[0].astype(F32)
    for s in range(1, in_ref.shape[0]):
        total += in_ref[s].astype(F32)
    out_ref[...] = total * factor


def after(x, *others):
    anywhere = pl.BlockSpec(memory_space=pl.ANY)
    return pl.pallas_call(
        lambda *refs: None,
        out_shape=jax.ShapeDtypeStruct(x.shape, x.dtype),
        in_specs=[anywhere] * (1 + len(others)),
        out_specs=anywhere,
        input_output_aliases={0: 0},
        compiler_params=pltpu.CompilerParams(vmem_limit_bytes=MIB),
    )(x, *others)


def ring(count, step):
    return [(i, (i + step) % count) for i in range(count)]


def on_device(fock_band, fock_slot_mask, orbital_slab, orbital_mask, result_mask):
    blocks, slots = fock_slot_mask.shape
    rows, columns = orbital_slab.shape
    size = rows // blocks
    half = columns // 2
    like = jax.ShapeDtypeStruct
    groups, wide, deep = lax.axis_size(ROWS), lax.axis_size("y"), lax.axis_size("z")
    plane = wide * deep
    piece = like((rows, half), BF16)
    h0, h1, panels = call(
        functools.partial(mask_kernel, size),
        (piece, piece, like((2, rows, half), BF16)),
        [HBM, HBM],
        [
            pltpu.SMEM(orbital_mask.shape[::-1], jnp.int32),
            pltpu.VMEM((rows, columns), BF16),
            pltpu.VMEM((2, rows, half), BF16),
            pltpu.SemaphoreType.DMA,
            pltpu.SemaphoreType.DMA((blocks // 2,)),
            pltpu.SemaphoreType.DMA((blocks // 2, 4)),
        ],
        limit=60 * MIB,
        place=HBM,
    )(orbital_mask.T, orbital_slab)
    swap = ring(2, 1)
    low0 = lax.ppermute(h0, ROWS, ring(groups, 1))
    high0 = lax.ppermute(h0, ROWS, ring(groups, groups - 1))
    ends = [(i, (i + plane) % groups) for i in range(groups) if i % plane in (0, plane - 1)]
    crossed = lax.ppermute(h1, ROWS, ends)
    far = lax.ppermute(panels, "xh", swap)
    near_panels = lax.ppermute(panels, "core", swap)
    held, mid0, mid1 = call(
        functools.partial(middle_kernel, size),
        (like((rows, slots * size), BF16), *[like((rows, half), F32)] * 2),
        [SMEM, VMEM, VMEM, VMEM],
        flops=2 * rows * rows * columns,
        moved=4 * rows * slots * size,
    )(fock_slot_mask, fock_band, h0, h1)
    up1, down1 = call(
        functools.partial(pick_kernel, (wide, deep)), (piece, piece), [VMEM, VMEM], moved=8 * rows * half
    )(h1, after(crossed, near_panels))
    within = [(i, i + 1 if (i + 1) % plane else i + 1 - plane) for i in range(groups)]
    low1 = lax.ppermute(up1, ROWS, within)
    high1 = lax.ppermute(down1, ROWS, [(b, a) for a, b in within])

    def near(h, mid, low, high, *first):
        width = half if h == 0 else columns
        return call(
            functools.partial(near_kernel, size, h),
            (like((rows, width), BF16), like((half, rows), BF16), like((4, half, half), BF16)),
            [SMEM] + [VMEM] * (7 + len(first)),
            flops=2 * rows * half * (2 * columns + (slots - blocks) * size),
            moved=8 * rows * columns,
        )(result_mask.T, held, mid, low, high, h0, h1, near_panels, *first)

    product0, flipped0, terms0 = near(0, mid0, low0, high0)
    product, flipped1, terms1 = near(1, mid1, low1, high1, product0)
    far = after(far, terms1)
    both = lax.ppermute(far, "core", swap)
    far_terms = call(
        far_kernel,
        like((2, columns, half), BF16),
        [VMEM] * 3,
        flops=4 * rows * half * columns,
        moved=8 * rows * half,
    )(flipped0, flipped1, far)
    terms = call(
        gather_kernel,
        like((groups // deep, columns, half), BF16),
        [VMEM] * 6,
        flops=4 * rows * half * columns,
        moved=8 * rows * columns,
    )(flipped0, flipped1, both, terms0, terms1, far_terms)
    terms = lax.all_to_all(terms, ("xl", "y"), 0, 0, tiled=True)
    part = call(first_sum_kernel, like((half, columns), BF16), [VMEM])(terms)
    part = part.reshape(deep, half // deep, columns)
    part = lax.all_to_all(part, "z", 0, 0, tiled=True)
    factor = 1.0 / math.sqrt(rows * groups)
    projected = call(
        functools.partial(last_sum_kernel, factor), like((half // deep, columns), F32), [VMEM]
    )(part)
    return (product, projected)


def solution(mesh):
    split = Mesh(mesh.devices.reshape(2, 2, 2, 4, 8), BLK + ROWS)
    placed = (P(ROWS, None), P(ROWS, None), P(ROWS, BLK), P(ROWS, BLK), P(ROWS, BLK))
    return jax.shard_map(
        on_device,
        mesh=split,
        in_specs=placed,
        out_specs=(P(ROWS, BLK), P(ROWS, BLK)),
        check_vma=False,
    )
```
